256 devices in a mesh: rep: 4 (over y_lo, core), dp: 64 (over z, x, y_hi).
Axes of the slice: x: 4, y: 4 (y_hi: 2, y_lo: 2; y = y_hi * 2 + y_lo), z: 8, core: 2. Of those that a mesh axis runs over, the one named last changes fastest.
Arguments:
- first_core: float32 [512, 512], P('dp'), may hold values from -6 to 6
- first_moment: float32 [512, 512], P('dp'), may hold values from -4 to 4
- first_second: float32 [512, 512], P('dp'), may hold values from 0.01 to 1
- mid_core: float32 [256, 131072], P('dp'), may hold values from -0.5 to 0.5
- mid_moment: float32 [256, 131072], P('dp'), may hold values from -4 to 4
- mid_second: float32 [256, 131072], P('dp'), may hold values from 0.01 to 1
- last_core: float32 [512, 512], P('dp'), may hold values from -0.5 to 0.5
- last_moment: float32 [512, 512], P('dp'), may hold values from -4 to 4
- last_second: float32 [512, 512], P('dp'), may hold values from 0.01 to 1
- cotangent: bfloat16 [4096, 128], P(('rep', 'dp')), may hold values from -6 to 6
- bag_lengths: int32 [256, 16], P(('rep', 'dp')), may hold values from 1 to 32, 256 in all within a row
- first_digit: int32 [65536], P(('rep', 'dp')), may hold values from 0 to 511
- mid_digit: int32 [65536, 1], P(('rep', 'dp')), may hold values from 0 to 255; in each aligned block of 256 rows (0 to 255, 256 to 511, ...) at most 2 rows name the same one
- last_digit: int32 [65536], P(('rep', 'dp')), may hold values from 0 to 511
Outputs:
- first_core_next: float32 [512, 512], P('dp')
- first_moment_next: float32 [512, 512], P('dp')
- first_second_next: float32 [512, 512], P('dp')
- mid_core_next: float32 [256, 131072], P('dp')
- mid_moment_next: float32 [256, 131072], P('dp')
- mid_second_next: float32 [256, 131072], P('dp')
- last_core_next: float32 [512, 512], P('dp')
- last_moment_next: float32 [512, 512], P('dp')
- last_second_next: float32 [512, 512], P('dp')
The draws below stay inside these ranges and needn't reach their ends.
Inputs may be any that keep to these rules, and one draw needn't show every extreme that they name: `mid_digit`: within each block of 256 lookups no middle digit appears more than 2 times, and in some block one digit appears exactly 2 times. `bag_lengths`: each row sums to 256; some entry of each row equals 32.
All inputs are finite; a program needn't handle non-finite values.
Results may differ from the reference program's by a relative error of at most 0.0056.
Values may be sent and summed in bfloat16 or wider, within the bound.
No kernel may reach another device: no remote copies, remote signals or barrier semaphores. Data moves between devices by JAX's collectives and lax.ppermute only.
A program may use at most 64 MiB of HBM per device.

```python
import math
import jax
import jax.numpy as jnp
import numpy as np
from jax import lax

N1 = 512
N2 = 256
N3 = 512
R = 128
D1 = 4
D2 = 8
D3 = 4
STEP = 20
SAMP_DEV = 16
D = 128
LK_DEV = 256
MOSTLEN = 32
CAP = 2
SAMPLES = 4096
LOOKUPS = 65536
N_REP = 4
N_DP = 64


def set_ends(array, rng, low, top_value):
    shape = array.shape
    spot = [jax.random.randint(jax.random.fold_in(rng, axis), (), 0, shape[axis]) for axis in range(len(shape))]
    array = array.at[tuple(spot)].set(low)
    longest = shape.index(max(shape))
    spot[longest] = (spot[longest] + 1) % shape[longest]
    return array.at[tuple(spot)].set(top_value)


def levels(own_key, shape, split, smallest, top_value):
    def one(dim, parts):
        steps = jax.random.uniform(jax.random.fold_in(jax.random.fold_in(own_key, 6), dim), (parts,), jnp.float32, smallest / len(split), top_value / len(split))
        return jnp.repeat(jnp.exp(steps), shape[dim] // parts).reshape((-1,) + (1,) * (len(shape) - dim - 1))

    gain = one(*split[0])
    for cut in split[1:]:
        gain = gain * one(*cut)
    return gain


def cumulative_ranks(count, slope):
    loads = [(1 << 20) // math.isqrt(rank ** slope) + 1 for rank in range(1, count + 1)]
    scale = 1 + sum(loads) // (1 << 30)
    return np.cumsum(np.array([max(1, weight // scale) for weight in loads]))


def ranked_ids(rng, shape, count, skew):
    listing = cumulative_ranks(count, skew)
    pick = jax.random.randint(jax.random.fold_in(rng, 1), shape, 0, int(listing[count - 1]))
    standing = jnp.searchsorted(jnp.asarray(listing, jnp.int32), pick, side="right")
    return jax.random.permutation(jax.random.fold_in(rng, 2), count)[standing].astype(jnp.int32)


def split_up(amount, total, bound, skew):
    loads = [(1 << 20) // math.isqrt(standing ** skew) + 1 for standing in range(2, amount + 1)]
    spare, given = total - bound - (amount - 1), [1] * (amount - 1)
    while spare > 0:
        candidates = [i for i in range(amount - 1) if given[i] < bound]
        mass, left = sum([loads[i] for i in candidates]), spare
        for i in candidates:
            addition = min(bound - given[i], max(1, left * loads[i] // mass), spare)
            given[i] = given[i] + addition
            spare = spare - addition
    return np.array([bound] + given)


def uneven_parts(rng, number_of, total, most, lean):
    if number_of == 2:
        one = jax.random.randint(rng, (), max(1, total - most), min(most, total - 1) + 1)
        return jnp.stack([one, total - one])
    tallies = jnp.asarray(split_up(number_of, total, most, lean), jnp.int32)
    couples = (number_of - 1) // 2
    giver, taker = tallies[1:1 + 2 * couples:2], tallies[2:2 + 2 * couples:2]
    room = jnp.minimum(giver - 1, most - taker)
    passed = jax.random.randint(jax.random.fold_in(rng, 1), (couples,), 0, 1 << 20) % (room + 1)
    tallies = tallies.at[1:1 + 2 * couples:2].set(giver - passed).at[2:2 + 2 * couples:2].set(taker + passed)
    return tallies[jax.random.permutation(jax.random.fold_in(rng, 2), number_of)]


def shared_out(rng, own, number, rows, number_of, top, most, skew):
    ranking = jax.random.permutation(rng, number_of)
    packed, usual = load_shares(number_of, rows * top, most, skew, True), load_shares(number_of, rows * top, most, skew, False)
    places = jnp.arange(number_of)

    def named(tallies, offset_by):
        used = int((tallies > 0).sum())
        fixed = max(1, used // 4)
        passed = fixed + (places - fixed + offset_by * (used - fixed)) % max(1, number_of - fixed)
        return jnp.zeros((number_of,), jnp.int32).at[ranking[jnp.where(places < fixed, places, passed)]].set(jnp.asarray(tallies, jnp.int32))

    tallies = jnp.where(number % 4 == 0, named(packed, number // 4), named(usual, number - number // 4 - 1))
    mixed = jax.random.permutation(jax.random.fold_in(own, 3), number_of)
    giver, sink = mixed[0:number_of // 2 * 2:2], mixed[1:number_of // 2 * 2:2]
    room = jnp.minimum(tallies[giver] - 1, most - tallies[sink]) // 2
    room = jnp.where((giver == ranking[0]) | (sink == ranking[0]) | (tallies[sink] == 0), 0, jnp.maximum(room, 0))
    passed = jax.random.randint(jax.random.fold_in(own, 4), (number_of // 2,), 0, 1 << 20) % (room + 1)
    tallies = tallies.at[giver].add(-passed).at[sink].add(passed)
    members = jnp.searchsorted(jnp.cumsum(tallies), jnp.arange(rows * top), side="right").astype(jnp.int32)
    listing = members.reshape(top, rows).T
    listing = listing[jax.random.permutation(jax.random.fold_in(own, 1), rows)]
    offset_by = jax.random.randint(jax.random.fold_in(own, 2), (rows, 1), 0, top)
    return jnp.take_along_axis(listing, (jnp.arange(top)[None, :] + offset_by) % top, axis=1)


def load_shares(amount, total, limit, slope, full):
    weights = [(1 << 20) // math.isqrt(rank ** slope) + 1 for rank in range(1, amount + 1)]
    largest = limit if full else min(limit, max(-(-total // amount), total * weights[0] // sum(weights)))
    least = 1 if total - largest >= amount - 1 else 0
    holding, rest = [largest] + [least] * (amount - 1), total - largest - least * (amount - 1)
    while rest > 0:
        candidates = [i for i in range(1, amount) if holding[i] < largest] or [i for i in range(1, amount) if holding[i] < limit]
        mass, budget = sum([weights[i] for i in candidates]), rest
        for i in candidates:
            addition = min(limit - holding[i], max(1, budget * weights[i] // mass), rest)
            holding[i] = holding[i] + addition
            rest = rest - addition
    return np.array(holding)


def gaussian(own_key, dims, deviation, bound, cuts=(), kind=jnp.bfloat16):
    values = jax.random.normal(own_key, dims, jnp.float32) * deviation
    if len(cuts) > 0:
        values = levels(own_key, dims, cuts, -0.22, 0.18) * values
    return jnp.clip(values, min=-bound, max=bound).astype(kind)


def setup_inputs(seed: int = 0) -> dict:
    key_of = jax.random.split(jax.random.key(seed), 15)
    first_core = gaussian(key_of[0], (N1, D1 * R), 1.0, 6.0, ((0, 64),), jnp.float32)
    first_moment = gaussian(key_of[1], (N1, D1 * R), 0.5, 4.0, ((0, 64),), jnp.float32)
    first_second = jnp.clip(jnp.exp(math.log(1.0) - 4.6051702 * jax.random.uniform(key_of[2], (N1, D1 * R), jnp.float32) ** levels(key_of[2], (N1, D1 * R), ((0, 64),), -0.2, 0.2)), 0.01, 1.0)
    mid_core = gaussian(key_of[3], (N2, R * D2 * R), R ** -0.5, 0.5, ((0, 64),), jnp.float32)
    mid_moment = gaussian(key_of[4], (N2, R * D2 * R), 0.5, 4.0, ((0, 64),), jnp.float32)
    mid_second = jnp.clip(jnp.exp(math.log(1.0) - 4.6051702 * jax.random.uniform(key_of[5], (N2, R * D2 * R), jnp.float32) ** levels(key_of[5], (N2, R * D2 * R), ((0, 64),), -0.2, 0.2)), 0.01, 1.0)
    last_core = gaussian(key_of[6], (N3, R * D3), R ** -0.5, 0.5, ((0, 64),), jnp.float32)
    last_moment = gaussian(key_of[7], (N3, R * D3), 0.5, 4.0, ((0, 64),), jnp.float32)
    last_second = jnp.clip(jnp.exp(math.log(1.0) - 4.6051702 * jax.random.uniform(key_of[8], (N3, R * D3), jnp.float32) ** levels(key_of[8], (N3, R * D3), ((0, 64),), -0.2, 0.2)), 0.01, 1.0)
    cotangent = gaussian(key_of[9], (SAMPLES, D), 1.0, 6.0, ((0, 256),))
    bag_lengths = jax.vmap(lambda own: uneven_parts(own, SAMP_DEV, LK_DEV, MOSTLEN, 1))(jax.random.split(key_of[10], (N_REP * N_DP))).reshape((N_REP * N_DP, SAMP_DEV)).astype(jnp.int32)
    first_digit = set_ends(ranked_ids(key_of[11], (LOOKUPS,), N1, 1), jax.random.fold_in(key_of[11], 3), 0, N1 - 1).astype(jnp.int32)
    mid_digit_keys = jax.random.split(jax.random.fold_in(key_of[12], 1), LOOKUPS // LK_DEV)
    mid_digit_turns = jax.random.permutation(jax.random.fold_in(key_of[12], 3), LOOKUPS // LK_DEV)
    mid_digit = jax.vmap(lambda own, number: shared_out(jax.random.fold_in(key_of[12], 2), own, number, LK_DEV, N2, 1, CAP, 1))(mid_digit_keys, mid_digit_turns).reshape((LOOKUPS, 1))
    last_digit = set_ends(ranked_ids(key_of[13], (LOOKUPS,), N3, 1), jax.random.fold_in(key_of[13], 3), 0, N3 - 1).astype(jnp.int32)
    return {"first_core": first_core, "first_moment": first_moment, "first_second": first_second, "mid_core": mid_core, "mid_moment": mid_moment, "mid_second": mid_second, "last_core": last_core, "last_moment": last_moment, "last_second": last_second, "cotangent": cotangent, "bag_lengths": bag_lengths, "first_digit": first_digit, "mid_digit": mid_digit, "last_digit": last_digit}


LEARN_RATE = 0.01
BETA_ONE = 0.9
BETA_TWO = 0.999
EPSILON = 1e-08

def adam_update(current, moment, second, gradient):
    moment_next = BETA_ONE * moment + (1.0 - BETA_ONE) * gradient
    second_next = BETA_TWO * second + (1.0 - BETA_TWO) * gradient * gradient
    corrected = moment_next / (1.0 - BETA_ONE ** STEP)
    spread = jnp.sqrt(second_next / (1.0 - BETA_TWO ** STEP))
    return (current - LEARN_RATE * corrected / (spread + EPSILON), moment_next, second_next)

def reference(first_core, first_moment, first_second, mid_core, mid_moment, mid_second, last_core, last_moment, last_second, cotangent, bag_lengths, first_digit, mid_digit, last_digit):
    blocks = bag_lengths.shape[0]
    look_count = first_digit.shape[0] // blocks
    positions = jnp.arange(look_count, dtype=jnp.int32)
    bag_ends = jnp.cumsum(bag_lengths, axis=1)
    sample_of = lax.optimization_barrier(jnp.sum((bag_ends[:, None, :] <= positions[None, :, None]).astype(jnp.int32), axis=2))
    sample_of = sample_of + (jnp.arange(blocks, dtype=jnp.int32) * SAMP_DEV)[:, None]
    lookup_grads = cotangent[sample_of.reshape(-1)]
    mid_rows = mid_digit[:, 0].reshape(blocks, look_count)

    def block_rank(row_ids):
        earlier = (row_ids[None, :] == row_ids[:, None]) & (positions[None, :] < positions[:, None])
        return lax.optimization_barrier(jnp.sum(earlier.astype(jnp.int32), axis=1))
    slot_rank = lax.map(block_rank, mid_rows)
    slot_index = (mid_rows * blocks + jnp.arange(blocks, dtype=jnp.int32)[:, None]) * CAP + slot_rank
    lookup_ids = jnp.arange(first_digit.shape[0], dtype=jnp.int32) + 1
    owner_of = jnp.zeros((N2 * blocks * CAP,), jnp.int32).at[slot_index.reshape(-1)].set(lookup_ids)
    owner_of = owner_of.reshape(N2, blocks * CAP)
    first_copy = first_core.astype(jnp.bfloat16)
    mid_copy = mid_core.astype(jnp.bfloat16)
    last_copy = last_core.astype(jnp.bfloat16)

    def row_step(totals, row_items):
        first_acc, last_acc = totals
        slot_owner, mid_row = row_items
        live_slot = slot_owner > 0
        picked = jnp.maximum(slot_owner - 1, 0)
        slot_count = slot_owner.shape[0]
        slot_grads = jnp.where(live_slot[:, None], lookup_grads[picked], jnp.zeros((), jnp.bfloat16))
        slot_first = jnp.where(live_slot, first_digit[picked], 0).astype(jnp.int32)
        slot_last = jnp.where(live_slot, last_digit[picked], 0).astype(jnp.int32)
        grad_cube = slot_grads.reshape(slot_count, D1, D2, D3).astype(jnp.float32)
        first_rows = first_copy[slot_first].reshape(slot_count, D1, R).astype(jnp.float32)
        last_rows = last_copy[slot_last].reshape(slot_count, R, D3).astype(jnp.float32)
        mid_cube = mid_row.reshape(R, D2, R).astype(jnp.float32)
        first_mix = jnp.einsum('kar,kabc->krbc', first_rows, grad_cube).astype(jnp.bfloat16)
        mid_term = jnp.einsum('krbc,ksc->rbs', first_mix.astype(jnp.float32), last_rows)
        tail_mix = jnp.einsum('rbs,ksc->krbc', mid_cube, last_rows).astype(jnp.bfloat16)
        first_term = jnp.einsum('kabc,krbc->kar', grad_cube, tail_mix.astype(jnp.float32))
        head_mix = jnp.einsum('kar,rbs->kabs', first_rows, mid_cube).astype(jnp.bfloat16)
        last_term = jnp.einsum('kabs,kabc->ksc', head_mix.astype(jnp.float32), grad_cube)
        first_acc = first_acc + jax.ops.segment_sum(first_term.reshape(slot_count, D1 * R), slot_first, num_segments=N1)
        last_acc = last_acc + jax.ops.segment_sum(last_term.reshape(slot_count, R * D3), slot_last, num_segments=N3)
        return ((first_acc, last_acc), mid_term.reshape(-1))
    start = (jnp.zeros((N1, D1 * R), jnp.float32), jnp.zeros((N3, R * D3), jnp.float32))
    (first_grad, last_grad), mid_grad = lax.scan(row_step, start, (owner_of, mid_copy))
    first_next = adam_update(first_core, first_moment, first_second, first_grad)
    mid_next = adam_update(mid_core, mid_moment, mid_second, mid_grad)
    last_next = adam_update(last_core, last_moment, last_second, last_grad)
    return (first_next[0], first_next[1], first_next[2], mid_next[0], mid_next[1], mid_next[2], last_next[0], last_next[1], last_next[2])
```

```python
from functools import partial

import jax
import jax.numpy as jnp
from jax import lax
from jax.experimental import pallas as pl
from jax.experimental.pallas import tpu as pltpu
from jax.sharding import PartitionSpec as P

N2 = 256
R = 128
D1 = 4
D2 = 8
D3 = 4
STEP = 20
CAP = 2
LANES = 128
N_SRC = 64
SLOTS = 512
PER_ROW = 128
CHUNK = 16

LEARN_RATE = 0.01
BETA_ONE = 0.9
BETA_TWO = 0.999
EPSILON = 1e-08

BF = jnp.bfloat16
F32 = jnp.float32
INTERPRET = False


def adam_update(current, moment, second, gradient):
    moment_next = BETA_ONE * moment + (1.0 - BETA_ONE) * gradient
    second_next = BETA_TWO * second + (1.0 - BETA_TWO) * gradient * gradient
    corrected = moment_next / (1.0 - BETA_ONE**STEP)
    spread = jnp.sqrt(second_next / (1.0 - BETA_TWO**STEP))
    return (current - LEARN_RATE * corrected / (spread + EPSILON), moment_next, second_next)


def iota(shape, axis):
    return lax.broadcasted_iota(jnp.int32, shape, axis)


def nn(a, b):
    return lax.dot_general(a, b, (((1,), (0,)), ((), ())), preferred_element_type=F32)


def nt(a, b):
    return lax.dot_general(a, b, (((1,), (1,)), ((), ())), preferred_element_type=F32)


def tn(a, b):
    return lax.dot_general(a, b, (((0,), (0,)), ((), ())), preferred_element_type=F32)


def ones_where(cond):
    return jnp.where(cond, 1.0, 0.0).astype(BF)


def split_two(x):
    hi = x.astype(BF)
    return hi, (x - hi.astype(F32)).astype(BF)


def pack_kernel(side_ref, mid_ref, first_ref, last_ref, bag_ref, cot_ref, fcore_ref, lcore_ref, out_ref):
    count = mid_ref.shape[1]
    mids = jnp.broadcast_to(mid_ref[...].astype(F32), (count, count))
    row, col = iota((count, count), 0), iota((count, count), 1)
    mid_column = jnp.sum(jnp.where(row == col, mids, 0.0), axis=1, keepdims=True)
    earlier = (mid_column == mids) & (row < col)
    rank = jnp.sum(jnp.where(earlier, 1.0, 0.0), axis=0, keepdims=True)
    slot = mid_ref[...] * CAP + rank.astype(jnp.int32)
    place = ones_where(iota((SLOTS, count), 0) == slot)

    samples = bag_ref.shape[1]
    lens = jnp.broadcast_to(bag_ref[...].astype(F32), (samples, samples))
    n_row, n_col = iota((samples, samples), 0), iota((samples, samples), 1)
    ends = jnp.sum(jnp.where(n_col <= n_row, lens, 0.0), axis=1, keepdims=True)
    starts = jnp.sum(jnp.where(n_col < n_row, lens, 0.0), axis=1, keepdims=True)
    position = iota((samples, count), 1).astype(F32)
    owner = ones_where((position >= starts) & (position < ends))
    slot_owner = nt(place, owner).astype(BF)
    out_ref[:, 0:LANES] = nn(slot_owner, cot_ref[...]).astype(BF)

    field = iota((LANES, count), 0)
    first, last = first_ref[...], last_ref[...]
    fields = jnp.where(field == 0, first // 32, 0)
    fields = jnp.where(field == 1, first % 32, fields)
    fields = jnp.where(field == 2, last // 32, fields)
    fields = jnp.where(field == 3, last % 32, fields)
    out_ref[:, LANES : 2 * LANES] = nt(place, fields.astype(F32).astype(BF)).astype(BF)

    side = side_ref[0]
    width = fcore_ref.shape[1]
    core = jnp.where(side == 0, fcore_ref[...], lcore_ref[...])
    core = jnp.concatenate([core, core], axis=0).astype(BF)
    dest = iota((width, width), 1)
    source = jnp.where(side == 0, dest, (dest % LANES) * D3 + dest // LANES)
    core = nn(core, ones_where(iota((width, width), 0) == source)).astype(BF)
    for p in range(SLOTS // 16):
        out_ref[p * 16 : p * 16 + 16, 2 * LANES : 2 * LANES + width] = core


def pack(side, mid_digit, first_digit, last_digit, bag, cot, first_core, last_core):
    vmem = pl.BlockSpec(memory_space=pltpu.VMEM)
    return pl.pallas_call(
        pack_kernel,
        out_shape=jax.ShapeDtypeStruct((SLOTS, 2 * LANES + first_core.shape[1]), BF),
        in_specs=[pl.BlockSpec(memory_space=pltpu.SMEM)] + [vmem] * 7,
        out_specs=vmem,
        interpret=INTERPRET,
        name="pack",
    )(side, mid_digit, first_digit, last_digit, bag, cot, first_core, last_core)


def terms_kernel(
    side_ref, mine_ref, theirs_ref, mid_ref,
    midgrad_ref, keep_ref, send_ref,
    cores, arows, lrows, grads, head, mix_hi, mix_lo, fterm, lterm, midm, asub, midf,
):
    side = side_ref[0]
    width = cores.shape[2]
    cores[side] = mine_ref[:, 2 * LANES :]
    cores[1 - side] = theirs_ref[:, 2 * LANES :]
    new = iota((SLOTS, SLOTS), 0)
    old = (new % 64) * 8 + (new // 128) * 2 + (new // 64) % 2
    lane = iota((SLOTS, SLOTS), 1)
    slots = nn(ones_where(lane == old), mine_ref[:, 0 : 2 * LANES])
    grads[...] = slots[:, 0:LANES]
    first = slots[:, LANES : LANES + 1] * 32.0 + slots[:, LANES + 1 : LANES + 2]
    last = slots[:, LANES + 2 : LANES + 3] * 32.0 + slots[:, LANES + 3 : LANES + 4]
    lane_f = lane.astype(F32)
    pick_first = ones_where(lane_f == first)
    pick_last = ones_where(lane_f == last)
    arows[...] = nn(pick_first, cores[0]).astype(BF)
    lrows[...] = nn(pick_last, cores[1])

    def load_row(m):
        for b in range(D2):
            midm[:, b * LANES : (b + 1) * LANES] = mid_ref[
                pl.ds(b * 4 + m, R, stride=4 * D2), :
            ].astype(BF)
        for a in range(D1):
            asub[a * PER_ROW : (a + 1) * PER_ROW, :] = arows[
                m * PER_ROW : (m + 1) * PER_ROW, a * R : (a + 1) * R
            ]

    for m in range(4):
        load_row(m)
        head[m * SLOTS : (m + 1) * SLOTS, :] = nn(asub[...], midm[...]).astype(BF)

    def step(t, carry):
        n0 = pl.multiple_of(t * CHUNK, CHUNK)
        m = t // (PER_ROW // CHUNK)
        k0 = n0 - m * PER_ROW
        g = grads[pl.ds(n0, CHUNK), :]
        rows = [lrows[pl.ds(n0, CHUNK), c * LANES : (c + 1) * LANES] for c in range(D3)]
        sums = [jnp.zeros((CHUNK, LANES), F32) for _ in range(D3)]
        for a in range(D1):
            base = pl.multiple_of(m * SLOTS + a * PER_ROW + k0, CHUNK)
            for b in range(D2):
                at = a * D2 * D3 + b * D3
                h = head[pl.ds(base, CHUNK), b * LANES : (b + 1) * LANES].astype(F32)
                mix = None
                for c in range(D3):
                    spread = jnp.broadcast_to(g[:, at + c : at + c + 1], (CHUNK, LANES))
                    part = spread * rows[c]
                    mix = part if mix is None else mix + part
                    sums[c] = sums[c] + spread * h
                hi, lo = split_two(mix)
                mix_hi[pl.ds(base, CHUNK), b * LANES : (b + 1) * LANES] = hi
                mix_lo[pl.ds(base, CHUNK), b * LANES : (b + 1) * LANES] = lo
        for c in range(D3):
            lterm[pl.ds(n0, CHUNK), c * LANES : (c + 1) * LANES] = sums[c]
        return carry

    lax.fori_loop(0, SLOTS // CHUNK, step, 0)

    for m in range(4):
        load_row(m)
        hi = mix_hi[m * SLOTS : (m + 1) * SLOTS, :]
        lo = mix_lo[m * SLOTS : (m + 1) * SLOTS, :]
        part = nt(hi, midm[...]) + nt(lo, midm[...])
        for a in range(D1):
            fterm[m * PER_ROW : (m + 1) * PER_ROW, a * R : (a + 1) * R] = part[
                a * PER_ROW : (a + 1) * PER_ROW, :
            ]
        grad = tn(asub[...], hi) + tn(asub[...], lo)
        for b in range(D2):
            midf[pl.ds(b * 4 + m, R, stride=4 * D2), :] = grad[:, b * LANES : (b + 1) * LANES]
    midgrad_ref[...] = midf[...].astype(BF)

    hi, lo = split_two(fterm[...])
    first_part = tn(pick_first, hi) + tn(pick_first, lo)
    hi, lo = split_two(lterm[...])
    last_part = tn(pick_last, hi) + tn(pick_last, lo)

    @pl.when(side == 0)
    def _():
        keep_ref[...] = first_part
        send_ref[...] = last_part

    @pl.when(side != 0)
    def _():
        keep_ref[...] = last_part
        send_ref[...] = first_part


def terms(side, mine, theirs, mid):
    vmem = pl.BlockSpec(memory_space=pltpu.VMEM)
    width = D1 * R
    return pl.pallas_call(
        terms_kernel,
        out_shape=(
            jax.ShapeDtypeStruct(mid.shape, BF),
            jax.ShapeDtypeStruct((SLOTS, width), F32),
            jax.ShapeDtypeStruct((SLOTS, width), F32),
        ),
        in_specs=[pl.BlockSpec(memory_space=pltpu.SMEM)] + [vmem] * 3,
        out_specs=(vmem, vmem, vmem),
        scratch_shapes=[
            pltpu.VMEM((2, SLOTS, width), BF),
            pltpu.VMEM((SLOTS, width), BF),
            pltpu.VMEM((SLOTS, width), F32),
            pltpu.VMEM((SLOTS, LANES), F32),
            pltpu.VMEM((4 * SLOTS, D2 * R), BF),
            pltpu.VMEM((4 * SLOTS, D2 * R), BF),
            pltpu.VMEM((4 * SLOTS, D2 * R), BF),
            pltpu.VMEM((SLOTS, width), F32),
            pltpu.VMEM((SLOTS, width), F32),
            pltpu.VMEM((R, D2 * R), BF),
            pltpu.VMEM((SLOTS, R), BF),
            pltpu.VMEM(mid.shape, F32),
        ],
        interpret=INTERPRET,
        name="terms",
    )(side, mine, theirs, mid)


def outer_kernel(side_ref, mine_ref, theirs_ref, *refs):
    side = side_ref[0]
    mine, theirs = mine_ref[...], theirs_ref[...]
    first_grad = jnp.where(side == 0, mine, theirs)
    last_grad = jnp.where(side == 0, theirs, mine)
    width = mine.shape[1]
    dest = iota((width, width), 1)
    source = (dest % D3) * LANES + dest // D3
    order = ones_where(iota((width, width), 0) == source)
    hi = last_grad.astype(BF)
    rest = last_grad - hi.astype(F32)
    low, lowest = split_two(rest)
    last_grad = nn(hi, order) + (nn(low, order) + nn(lowest, order))
    f_next = adam_update(refs[0][...], refs[1][...], refs[2][...], first_grad)
    l_next = adam_update(refs[3][...], refs[4][...], refs[5][...], last_grad)
    for ref, value in zip(refs[6:], f_next + l_next):
        ref[...] = value


def outer_step(side, mine, theirs, states):
    vmem = pl.BlockSpec(memory_space=pltpu.VMEM)
    return pl.pallas_call(
        outer_kernel,
        out_shape=tuple(jax.ShapeDtypeStruct(mine.shape, F32) for _ in range(6)),
        in_specs=[pl.BlockSpec(memory_space=pltpu.SMEM)] + [vmem] * 8,
        out_specs=(vmem,) * 6,
        interpret=INTERPRET,
        name="outer",
    )(side, mine, theirs, *states)


def row_tiles(x):
    return x.reshape(4, D2 * R, LANES).transpose(1, 0, 2).reshape(4 * D2 * R, LANES)


def untile(x):
    return x.reshape(D2 * R, 4, LANES).transpose(1, 0, 2).reshape(4, D2 * R * LANES)


CORE_SWAP = ((0, 1), (1, 0), (2, 3), (3, 2))
CHIP_SWAP = ((0, 2), (2, 0), (1, 3), (3, 1))


def local(
    first_core,
    first_moment,
    first_second,
    mid_core,
    mid_moment,
    mid_second,
    last_core,
    last_moment,
    last_second,
    cotangent,
    bag_lengths,
    first_digit,
    mid_digit,
    last_digit,
):
    side = (lax.axis_index("rep") % 2).astype(jnp.int32).reshape(1)
    packed = pack(
        side,
        mid_digit.reshape(1, -1),
        first_digit.reshape(1, -1),
        last_digit.reshape(1, -1),
        bag_lengths,
        cotangent,
        first_core,
        last_core,
    )
    mine = lax.all_to_all(packed, "dp", split_axis=0, concat_axis=0, tiled=True)
    theirs = lax.ppermute(mine, "rep", CORE_SWAP)
    mid_part, keep, send = terms(side, mine, theirs, row_tiles(mid_core))

    other = lax.ppermute(send, "rep", CORE_SWAP)
    share = lax.all_to_all(
        (keep + other).astype(BF), "dp", split_axis=0, concat_axis=0, tiled=True
    )
    share = jnp.sum(share.reshape(N_SRC, -1, share.shape[1]).astype(F32), axis=0)

    half_rows = mid_part.shape[0] // 2
    mid_other = lax.ppermute(mid_part, "rep", CORE_SWAP)
    mid_chip = (mid_part.astype(F32) + mid_other.astype(F32)).astype(BF)
    half = lax.dynamic_slice_in_dim(mid_chip, side[0] * half_rows, half_rows, axis=0)
    far_half = lax.ppermute(half, "rep", CHIP_SWAP)
    far_rest = lax.ppermute(far_half, "rep", CORE_SWAP)
    far = jnp.where(
        side[0] == 0,
        jnp.concatenate([far_half, far_rest], axis=0),
        jnp.concatenate([far_rest, far_half], axis=0),
    )
    mid_grad = mid_chip.astype(F32) + far.astype(F32)
    mid_next = adam_update(row_tiles(mid_core), row_tiles(mid_moment), row_tiles(mid_second), mid_grad)
    mid_next = tuple(untile(x) for x in mid_next)

    share = share + lax.ppermute(share, "rep", CHIP_SWAP)
    other_share = lax.ppermute(share, "rep", CORE_SWAP)
    outer = outer_step(
        side,
        share,
        other_share,
        (first_core, first_moment, first_second, last_core, last_moment, last_second),
    )
    return outer[:3] + mid_next + outer[3:]


def solution(mesh):
    rows = P("dp", None)
    spread = P(("rep", "dp"), None)
    flat = P(("rep", "dp"))
    return jax.shard_map(
        local,
        mesh=mesh,
        in_specs=(rows,) * 9 + (spread, spread, flat, spread, flat),
        out_specs=(rows,) * 9,
        check_vma=False,
    )
```

```python
import jax
import jax.numpy as jnp
from jax import lax
from jax.experimental import pallas as pl
from jax.experimental.pallas import tpu as pltpu
from jax.sharding import PartitionSpec as P


R = 128
D1 = 4
D2 = 8
D3 = 4
STEP = 20
CAP = 2
LANES = 128
N_SRC = 64
SLOTS = 512
GROUP = 64

LEARN_RATE = 0.01
BETA_ONE = 0.9
BETA_TWO = 0.999
EPSILON = 1e-08

BF = jnp.bfloat16
F32 = jnp.float32
INTERPRET = False


def adam_update(current, moment, second, gradient):
    moment_next = BETA_ONE * moment + (1.0 - BETA_ONE) * gradient
    second_next = BETA_TWO * second + (1.0 - BETA_TWO) * gradient * gradient
    corrected = moment_next / (1.0 - BETA_ONE**STEP)
    spread = jnp.sqrt(second_next / (1.0 - BETA_TWO**STEP))
    return (current - LEARN_RATE * corrected / (spread + EPSILON), moment_next, second_next)


def iota(shape, axis):
    return lax.broadcasted_iota(jnp.int32, shape, axis)


def nn(a, b):
    return lax.dot_general(a, b, (((1,), (0,)), ((), ())), preferred_element_type=F32)


def nt(a, b):
    return lax.dot_general(a, b, (((1,), (1,)), ((), ())), preferred_element_type=F32)


def tn(a, b):
    return lax.dot_general(a, b, (((0,), (0,)), ((), ())), preferred_element_type=F32)


def ones_where(cond):
    return jnp.where(cond, 1.0, 0.0).astype(BF)


def split_two(x):
    hi = x.astype(BF)
    return hi, (x - hi.astype(F32)).astype(BF)


def pack_kernel(side_ref, mid_ref, first_ref, last_ref, bag_ref, cot_ref, fcore_ref, lcore_ref, out_ref):
    count = mid_ref.shape[1]
    mids = jnp.broadcast_to(mid_ref[...].astype(F32), (count, count))
    row, col = iota((count, count), 0), iota((count, count), 1)
    mid_column = jnp.sum(jnp.where(row == col, mids, 0.0), axis=1, keepdims=True)
    earlier = (mid_column == mids) & (row < col)
    rank = jnp.sum(jnp.where(earlier, 1.0, 0.0), axis=0, keepdims=True)
    slot = mid_ref[...] * CAP + rank.astype(jnp.int32)
    place = ones_where(iota((SLOTS, count), 0) == slot)

    samples = bag_ref.shape[1]
    lens = jnp.broadcast_to(bag_ref[...].astype(F32), (samples, samples))
    n_row, n_col = iota((samples, samples), 0), iota((samples, samples), 1)
    ends = jnp.sum(jnp.where(n_col <= n_row, lens, 0.0), axis=1, keepdims=True)
    starts = jnp.sum(jnp.where(n_col < n_row, lens, 0.0), axis=1, keepdims=True)
    position = iota((samples, count), 1).astype(F32)
    owner = ones_where((position >= starts) & (position < ends))
    slot_owner = nt(place, owner).astype(BF)
    out_ref[:, 0:LANES] = nn(slot_owner, cot_ref[...]).astype(BF)

    field = iota((LANES, count), 0)
    first, last = first_ref[...], last_ref[...]
    fields = jnp.where(field == 0, first // 32, 0)
    fields = jnp.where(field == 1, first % 32, fields)
    fields = jnp.where(field == 2, last // 32, fields)
    fields = jnp.where(field == 3, last % 32, fields)
    out_ref[:, LANES : 2 * LANES] = nt(place, fields.astype(F32).astype(BF)).astype(BF)

    side = side_ref[0]
    width = fcore_ref.shape[1]
    core = jnp.where(side == 0, fcore_ref[...], lcore_ref[...])
    core = jnp.concatenate([core, core], axis=0).astype(BF)
    dest = iota((width, width), 1)
    source = jnp.where(side == 0, dest, (dest % LANES) * D3 + dest // LANES)
    core = nn(core, ones_where(iota((width, width), 0) == source)).astype(BF)
    for p in range(SLOTS // 16):
        out_ref[p * 16 : p * 16 + 16, 2 * LANES : 2 * LANES + width] = core


def pack(side, mid_digit, first_digit, last_digit, bag, cot, first_core, last_core):
    vmem = pl.BlockSpec(memory_space=pltpu.VMEM)
    return pl.pallas_call(
        pack_kernel,
        out_shape=jax.ShapeDtypeStruct((SLOTS, 2 * LANES + first_core.shape[1]), BF),
        in_specs=[pl.BlockSpec(memory_space=pltpu.SMEM)] + [vmem] * 7,
        out_specs=vmem,
        interpret=INTERPRET,
        name="pack",
    )(side, mid_digit, first_digit, last_digit, bag, cot, first_core, last_core)


def terms_kernel(
    side_ref, mine_ref, theirs_ref, mid_ref,
    midgrad_ref, keep_ref, send_ref,
    cores, lrows, pick, diag, mix_hi, mix_lo, fterm, lterm, midm, asub, midf,
):
    side = side_ref[0]
    cores[side] = mine_ref[:, 2 * LANES :]
    cores[1 - side] = theirs_ref[:, 2 * LANES :]
    up, across = iota((SLOTS, SLOTS), 0), iota((SLOTS, SLOTS), 1)
    slots = nn(ones_where(across == (up % GROUP) * 8 + up // GROUP), mine_ref[:, 0 : 2 * LANES])
    grads = slots[:, 0:LANES].astype(BF)
    first = slots[:, LANES : LANES + 1] * 32.0 + slots[:, LANES + 1 : LANES + 2]
    last = slots[:, LANES + 2 : LANES + 3] * 32.0 + slots[:, LANES + 3 : LANES + 4]
    across_f = across.astype(F32)
    pick_first = ones_where(across_f == first)
    pick_last = ones_where(across_f == last)
    arows = nn(pick_first, cores[0]).astype(BF)
    last_rows = nn(pick_last, cores[1]).astype(BF)
    for q in range(8):
        for c in range(D3):
            lrows[q, c * GROUP : (c + 1) * GROUP, :] = last_rows[
                q * GROUP : (q + 1) * GROUP, c * LANES : (c + 1) * LANES
            ]
        for a in range(D1):
            asub[q, a * GROUP : (a + 1) * GROUP, :] = arows[
                q * GROUP : (q + 1) * GROUP, a * R : (a + 1) * R
            ]

    pick[...] = jnp.zeros(pick.shape, BF)
    tile_row, tile_lane = iota((16, LANES), 0), iota((16, LANES), 1)
    for i in range(2 * D1 * D2):
        pick[i, (i // 8) * 16 : (i // 8) * 16 + 16, :] = ones_where(
            tile_row == 2 * (i % 8) + tile_lane // GROUP
        )
    own = ones_where(iota((SLOTS, 2 * LANES), 0) % GROUP == iota((SLOTS, 2 * LANES), 1) % GROUP)

    def spread(ab, carry):
        pair = jnp.concatenate([pick[2 * ab], pick[2 * ab + 1]], axis=1)
        value = nn(grads, pair).astype(BF) * own
        diag[0, ab] = value[:, 0:LANES]
        diag[1, ab] = value[:, LANES:]
        return carry

    lax.fori_loop(0, D1 * D2, spread, 0)

    for m in range(4):
        for b in range(D2):
            midm[m, b] = mid_ref[pl.ds(b * 4 + m, R, stride=4 * D2), :].astype(BF)

    def group(q, carry):
        here = pl.ds(pl.multiple_of(q * GROUP, GROUP), GROUP)
        m = q // 2
        left = asub[q]
        weights = lrows[q]
        total = None
        for b in range(D2):
            head = lax.dot_general(
                midm[m, b], left, (((0,), (1,)), ((), ())), preferred_element_type=F32
            ).astype(BF)
            block = jnp.concatenate(
                [
                    jnp.concatenate([diag[h, a * D2 + b, here, :] for a in range(D1)], axis=0)
                    for h in range(2)
                ],
                axis=1,
            )
            part = nn(head, block)
            total = part if total is None else total + part
            hi, lo = split_two(nn(block, weights))
            there = pl.ds(pl.multiple_of(q * D1 * GROUP, D1 * GROUP), D1 * GROUP)
            mix_hi[b, there, :] = hi
            mix_lo[b, there, :] = lo
        total = total.T
        for c in range(D3):
            lterm[c, here, :] = total[c * GROUP : (c + 1) * GROUP, :]
        return carry

    lax.fori_loop(0, 8, group, 0)

    for m in range(4):
        span = slice(m * SLOTS, (m + 1) * SLOTS)
        left = jnp.concatenate([asub[2 * m], asub[2 * m + 1]], axis=0)
        part = None
        for b in range(0, D2, 2):
            hi = jnp.concatenate([mix_hi[b, span, :], mix_hi[b + 1, span, :]], axis=1)
            lo = jnp.concatenate([mix_lo[b, span, :], mix_lo[b + 1, span, :]], axis=1)
            pair = jnp.concatenate([midm[m, b], midm[m, b + 1]], axis=1)
            term = nt(jnp.concatenate([hi, lo], axis=1), jnp.concatenate([pair, pair], axis=1))
            part = term if part is None else part + term
            grad = tn(left, hi) + tn(left, lo)
            midf[pl.ds(b * 4 + m, R, stride=4 * D2), :] = grad[:, 0:LANES]
            midf[pl.ds((b + 1) * 4 + m, R, stride=4 * D2), :] = grad[:, LANES:]
        for q in range(2):
            for a in range(D1):
                fterm[a, (2 * m + q) * GROUP : (2 * m + q + 1) * GROUP, :] = part[
                    (q * D1 + a) * GROUP : (q * D1 + a + 1) * GROUP, :
                ]
    midgrad_ref[...] = midf[...].astype(BF)

    hi, lo = split_two(jnp.concatenate([fterm[a] for a in range(D1)], axis=1))
    first_part = tn(pick_first, hi) + tn(pick_first, lo)
    hi, lo = split_two(jnp.concatenate([lterm[c] for c in range(D3)], axis=1))
    last_part = tn(pick_last, hi) + tn(pick_last, lo)

    @pl.when(side == 0)
    def _():
        keep_ref[...] = first_part
        send_ref[...] = last_part

    @pl.when(side != 0)
    def _():
        keep_ref[...] = last_part
        send_ref[...] = first_part


def terms(side, mine, theirs, mid):
    vmem = pl.BlockSpec(memory_space=pltpu.VMEM)
    width = D1 * R
    return pl.pallas_call(
        terms_kernel,
        out_shape=(
            jax.ShapeDtypeStruct(mid.shape, BF),
            jax.ShapeDtypeStruct((SLOTS, width), F32),
            jax.ShapeDtypeStruct((SLOTS, width), F32),
        ),
        in_specs=[pl.BlockSpec(memory_space=pltpu.SMEM)] + [vmem] * 3,
        out_specs=(vmem, vmem, vmem),
        scratch_shapes=[
            pltpu.VMEM((2, SLOTS, width), BF),
            pltpu.VMEM((8, D3 * GROUP, LANES), BF),
            pltpu.VMEM((2 * D1 * D2, LANES, LANES), BF),
            pltpu.VMEM((2, D1 * D2, SLOTS, LANES), BF),
            pltpu.VMEM((D2, 4 * SLOTS, LANES), BF),
            pltpu.VMEM((D2, 4 * SLOTS, LANES), BF),
            pltpu.VMEM((D1, SLOTS, LANES), F32),
            pltpu.VMEM((D3, SLOTS, LANES), F32),
            pltpu.VMEM((4, D2, R, LANES), BF),
            pltpu.VMEM((8, D1 * GROUP, R), BF),
            pltpu.VMEM(mid.shape, F32),
        ],
        interpret=INTERPRET,
        name="terms",
    )(side, mine, theirs, mid)


def outer_kernel(side_ref, mine_ref, theirs_ref, *refs):
    side = side_ref[0]
    mine, theirs = mine_ref[...], theirs_ref[...]
    first_grad = jnp.where(side == 0, mine, theirs)
    last_grad = jnp.where(side == 0, theirs, mine)
    width = mine.shape[1]
    dest = iota((width, width), 1)
    source = (dest % D3) * LANES + dest // D3
    order = ones_where(iota((width, width), 0) == source)
    hi = last_grad.astype(BF)
    rest = last_grad - hi.astype(F32)
    low, lowest = split_two(rest)
    last_grad = nn(hi, order) + (nn(low, order) + nn(lowest, order))
    f_next = adam_update(refs[0][...], refs[1][...], refs[2][...], first_grad)
    l_next = adam_update(refs[3][...], refs[4][...], refs[5][...], last_grad)
    for ref, value in zip(refs[6:], f_next + l_next):
        ref[...] = value


def outer_step(side, mine, theirs, states):
    vmem = pl.BlockSpec(memory_space=pltpu.VMEM)
    return pl.pallas_call(
        outer_kernel,
        out_shape=tuple(jax.ShapeDtypeStruct(mine.shape, F32) for _ in range(6)),
        in_specs=[pl.BlockSpec(memory_space=pltpu.SMEM)] + [vmem] * 8,
        out_specs=(vmem,) * 6,
        interpret=INTERPRET,
        name="outer",
    )(side, mine, theirs, *states)


def row_tiles(x):
    return x.reshape(4, D2 * R, LANES).transpose(1, 0, 2).reshape(4 * D2 * R, LANES)


def untile(x):
    return x.reshape(D2 * R, 4, LANES).transpose(1, 0, 2).reshape(4, D2 * R * LANES)


CORE_SWAP = ((0, 1), (1, 0), (2, 3), (3, 2))
CHIP_SWAP = ((0, 2), (2, 0), (1, 3), (3, 1))


def local(
    first_core,
    first_moment,
    first_second,
    mid_core,
    mid_moment,
    mid_second,
    last_core,
    last_moment,
    last_second,
    cotangent,
    bag_lengths,
    first_digit,
    mid_digit,
    last_digit,
):
    side = (lax.axis_index("rep") % 2).astype(jnp.int32).reshape(1)
    packed = pack(
        side,
        mid_digit.reshape(1, -1),
        first_digit.reshape(1, -1),
        last_digit.reshape(1, -1),
        bag_lengths,
        cotangent,
        first_core,
        last_core,
    )
    mine = lax.all_to_all(packed, "dp", split_axis=0, concat_axis=0, tiled=True)
    theirs = lax.ppermute(mine, "rep", CORE_SWAP)
    mid_part, keep, send = terms(side, mine, theirs, row_tiles(mid_core))

    mid_other = lax.ppermute(mid_part, "rep", CORE_SWAP)
    other = lax.ppermute(send, "rep", CORE_SWAP)
    half_rows = mid_part.shape[0] // 2
    mid_chip = (mid_part.astype(F32) + mid_other.astype(F32)).astype(BF)
    half = lax.dynamic_slice_in_dim(mid_chip, side[0] * half_rows, half_rows, axis=0)
    half, chip_sum = lax.optimization_barrier((half, (keep + other).astype(BF)))
    far_half = lax.ppermute(half, "rep", CHIP_SWAP)
    share = lax.all_to_all(chip_sum, "dp", split_axis=0, concat_axis=0, tiled=True)
    far_rest = lax.ppermute(far_half, "rep", CORE_SWAP)
    far = jnp.where(
        side[0] == 0,
        jnp.concatenate([far_half, far_rest], axis=0),
        jnp.concatenate([far_rest, far_half], axis=0),
    )
    mid_grad = mid_chip.astype(F32) + far.astype(F32)
    mid_next = adam_update(row_tiles(mid_core), row_tiles(mid_moment), row_tiles(mid_second), mid_grad)
    share, *mid_next = lax.optimization_barrier((share, *mid_next))
    mid_next = tuple(untile(x) for x in mid_next)
    share = jnp.sum(share.reshape(N_SRC, -1, share.shape[1]).astype(F32), axis=0)

    share = share + lax.ppermute(share, "rep", CHIP_SWAP)
    other_share = lax.ppermute(share, "rep", CORE_SWAP)
    outer = outer_step(
        side,
        share,
        other_share,
        (first_core, first_moment, first_second, last_core, last_moment, last_second),
    )
    return outer[:3] + mid_next + outer[3:]


def solution(mesh):
    rows = P("dp", None)
    spread = P(("rep", "dp"), None)
    flat = P(("rep", "dp"))
    return jax.shard_map(
        local,
        mesh=mesh,
        in_specs=(rows,) * 9 + (spread, spread, flat, spread, flat),
        out_specs=(rows,) * 9,
        check_vma=False,
    )
```

```python
import jax
import jax.numpy as jnp
from jax import lax
from jax.experimental import pallas as pl
from jax.experimental.pallas import tpu as pltpu
from jax.sharding import PartitionSpec as P


R = 128
D1 = 4
D2 = 8
D3 = 4
STEP = 20
CAP = 2
LANES = 128
N_SRC = 64
SLOTS = 512
GROUP = 64

LEARN_RATE = 0.01
BETA_ONE = 0.9
BETA_TWO = 0.999
EPSILON = 1e-08

BF = jnp.bfloat16
F32 = jnp.float32
INTERPRET = False


def adam_update(current, moment, second, gradient):
    moment_next = BETA_ONE * moment + (1.0 - BETA_ONE) * gradient
    second_next = BETA_TWO * second + (1.0 - BETA_TWO) * gradient * gradient
    corrected = moment_next / (1.0 - BETA_ONE**STEP)
    spread = jnp.sqrt(second_next / (1.0 - BETA_TWO**STEP))
    return (current - LEARN_RATE * corrected / (spread + EPSILON), moment_next, second_next)


def iota(shape, axis):
    return lax.broadcasted_iota(jnp.int32, shape, axis)


def nn(a, b):
    return lax.dot_general(a, b, (((1,), (0,)), ((), ())), preferred_element_type=F32)


def nt(a, b):
    return lax.dot_general(a, b, (((1,), (1,)), ((), ())), preferred_element_type=F32)


def tn(a, b):
    return lax.dot_general(a, b, (((0,), (0,)), ((), ())), preferred_element_type=F32)


def ones_where(cond):
    return jnp.where(cond, 1.0, 0.0).astype(BF)


def split_two(x):
    hi = x.astype(BF)
    return hi, (x - hi.astype(F32)).astype(BF)


def pack_kernel(side_ref, mid_ref, first_ref, last_ref, bag_ref, cot_ref, fcore_ref, lcore_ref, out_ref):
    count = mid_ref.shape[1]
    mids = jnp.broadcast_to(mid_ref[...].astype(F32), (count, count))
    row, col = iota((count, count), 0), iota((count, count), 1)
    mid_column = jnp.sum(jnp.where(row == col, mids, 0.0), axis=1, keepdims=True)
    earlier = (mid_column == mids) & (row < col)
    rank = jnp.sum(jnp.where(earlier, 1.0, 0.0), axis=0, keepdims=True)
    slot = mid_ref[...] * CAP + rank.astype(jnp.int32)
    place = ones_where(iota((SLOTS, count), 0) == slot)

    samples = bag_ref.shape[1]
    lens = jnp.broadcast_to(bag_ref[...].astype(F32), (samples, samples))
    n_row, n_col = iota((samples, samples), 0), iota((samples, samples), 1)
    ends = jnp.sum(jnp.where(n_col <= n_row, lens, 0.0), axis=1, keepdims=True)
    starts = jnp.sum(jnp.where(n_col < n_row, lens, 0.0), axis=1, keepdims=True)
    position = iota((samples, count), 1).astype(F32)
    owner = ones_where((position >= starts) & (position < ends))
    slot_owner = nt(place, owner).astype(BF)
    out_ref[:, 0:LANES] = nn(slot_owner, cot_ref[...]).astype(BF)

    field = iota((LANES, count), 0)
    first, last = first_ref[...], last_ref[...]
    fields = jnp.where(field == 0, first // 32, 0)
    fields = jnp.where(field == 1, first % 32, fields)
    fields = jnp.where(field == 2, last // 32, fields)
    fields = jnp.where(field == 3, last % 32, fields)
    out_ref[:, LANES : 2 * LANES] = nt(place, fields.astype(F32).astype(BF)).astype(BF)

    side = side_ref[0]
    width = fcore_ref.shape[1]
    core = jnp.where(side == 0, fcore_ref[...], lcore_ref[...])
    core = jnp.concatenate([core, core], axis=0).astype(BF)
    dest = iota((width, width), 1)
    source = jnp.where(side == 0, dest, (dest % LANES) * D3 + dest // LANES)
    core = nn(core, ones_where(iota((width, width), 0) == source)).astype(BF)
    for p in range(SLOTS // 16):
        out_ref[p * 16 : p * 16 + 16, 2 * LANES : 2 * LANES + width] = core


def pack(side, mid_digit, first_digit, last_digit, bag, cot, first_core, last_core):
    vmem = pl.BlockSpec(memory_space=pltpu.VMEM)
    return pl.pallas_call(
        pack_kernel,
        out_shape=jax.ShapeDtypeStruct((SLOTS, 2 * LANES + first_core.shape[1]), BF),
        in_specs=[pl.BlockSpec(memory_space=pltpu.SMEM)] + [vmem] * 7,
        out_specs=vmem,
        interpret=INTERPRET,
        name="pack",
    )(side, mid_digit, first_digit, last_digit, bag, cot, first_core, last_core)


def terms_kernel(
    side_ref, mine_ref, theirs_ref, mid_ref,
    midkeep_ref, midsend_ref, keep_ref, send_ref,
    cores, lrows, pick, diag, mix_hi, mix_lo, outer, chosen, asub,
):
    side = side_ref[0]
    cores[side] = mine_ref[:, 2 * LANES :]
    cores[1 - side] = theirs_ref[:, 2 * LANES :]
    up, across = iota((SLOTS, SLOTS), 0), iota((SLOTS, SLOTS), 1)
    slots = nn(ones_where(across == (up % GROUP) * 8 + up // GROUP), mine_ref[:, 0 : 2 * LANES])
    grads = slots[:, 0:LANES].astype(BF)
    first = slots[:, LANES : LANES + 1] * 32.0 + slots[:, LANES + 1 : LANES + 2]
    last = slots[:, LANES + 2 : LANES + 3] * 32.0 + slots[:, LANES + 3 : LANES + 4]
    across_f = across.astype(F32)
    pick_first = ones_where(across_f == first)
    pick_last = ones_where(across_f == last)
    chosen[side] = pick_first
    chosen[1 - side] = pick_last
    arows = nn(pick_first, cores[0]).astype(BF)
    last_rows = nn(pick_last, cores[1]).astype(BF)
    for q in range(8):
        for c in range(D3):
            lrows[q, c * GROUP : (c + 1) * GROUP, :] = last_rows[
                q * GROUP : (q + 1) * GROUP, c * LANES : (c + 1) * LANES
            ]
        for a in range(D1):
            asub[q, a * GROUP : (a + 1) * GROUP, :] = arows[
                q * GROUP : (q + 1) * GROUP, a * R : (a + 1) * R
            ]

    pick[...] = jnp.zeros(pick.shape, BF)
    tile_row, tile_lane = iota((16, LANES), 0), iota((16, LANES), 1)
    for i in range(2 * D1 * D2):
        pick[i, (i // 8) * 16 : (i // 8) * 16 + 16, :] = ones_where(
            tile_row == 2 * (i % 8) + tile_lane // GROUP
        )
    own = ones_where(iota((SLOTS, 2 * LANES), 0) % GROUP == iota((SLOTS, 2 * LANES), 1) % GROUP)

    def spread(step, carry):
        for part in range(8):
            ab = step * 8 + part
            pair = jnp.concatenate([pick[2 * ab], pick[2 * ab + 1]], axis=1)
            value = nn(grads, pair).astype(BF) * own
            diag[0, ab] = value[:, 0:LANES]
            diag[1, ab] = value[:, LANES:]
        return carry

    lax.fori_loop(0, D1 * D2 // 8, spread, 0)

    def group(q, carry):
        here = pl.ds(pl.multiple_of(q * GROUP, GROUP), GROUP)
        m = q // 2
        left = asub[q]
        weights = lrows[q]
        total = None
        for b in range(D2):
            head = lax.dot_general(
                mid_ref[m, b], left, (((0,), (1,)), ((), ())), preferred_element_type=F32
            ).astype(BF)
            block = jnp.concatenate(
                [
                    jnp.concatenate([diag[h, a * D2 + b, here, :] for a in range(D1)], axis=0)
                    for h in range(2)
                ],
                axis=1,
            )
            part = nn(head, block)
            total = part if total is None else total + part
            hi, lo = split_two(nn(block, weights))
            there = pl.ds(pl.multiple_of(q * D1 * GROUP, D1 * GROUP), D1 * GROUP)
            mix_hi[b, there, :] = hi
            mix_lo[b, there, :] = lo
        total = total.T
        for c in range(D3):
            outer[1 - side, c, here, :] = total[c * GROUP : (c + 1) * GROUP, :]
        return carry

    lax.fori_loop(0, 8, group, 0)

    for n in range(4):
        half = side if n < 2 else 1 - side
        m = half * 2 + n % 2
        grad_ref = midkeep_ref if n < 2 else midsend_ref
        span = pl.ds(pl.multiple_of(m * SLOTS, SLOTS), SLOTS)
        left = jnp.concatenate([asub[2 * m], asub[2 * m + 1]], axis=0)
        part = None
        for b in range(0, D2, 2):
            hi = jnp.concatenate([mix_hi[b, span, :], mix_hi[b + 1, span, :]], axis=1)
            lo = jnp.concatenate([mix_lo[b, span, :], mix_lo[b + 1, span, :]], axis=1)
            pair = jnp.concatenate([mid_ref[m, b], mid_ref[m, b + 1]], axis=1)
            term = nt(jnp.concatenate([hi, lo], axis=1), jnp.concatenate([pair, pair], axis=1))
            part = term if part is None else part + term
            grad = tn(left, hi)
            grad_ref[n % 2, b] = grad[:, 0:LANES]
            grad_ref[n % 2, b + 1] = grad[:, LANES:]
        for q in range(2):
            for a in range(D1):
                here = pl.ds(pl.multiple_of((2 * m + q) * GROUP, GROUP), GROUP)
                outer[side, a, here, :] = part[(q * D1 + a) * GROUP : (q * D1 + a + 1) * GROUP, :]

    for n, ref in ((1, send_ref), (0, keep_ref)):
        for a in range(0, D1, 2):
            hi, lo = split_two(jnp.concatenate([outer[n, a], outer[n, a + 1]], axis=1))
            ref[:, a * LANES : (a + 2) * LANES] = tn(chosen[n], hi) + tn(chosen[n], lo)


def terms(side, mine, theirs, mid):
    vmem = pl.BlockSpec(memory_space=pltpu.VMEM)
    width = D1 * R
    half = (2, D2, R, LANES)
    return pl.pallas_call(
        terms_kernel,
        out_shape=(
            jax.ShapeDtypeStruct(half, F32),
            jax.ShapeDtypeStruct(half, F32),
            jax.ShapeDtypeStruct((SLOTS, width), F32),
            jax.ShapeDtypeStruct((SLOTS, width), F32),
        ),
        in_specs=[pl.BlockSpec(memory_space=pltpu.SMEM)] + [vmem] * 3,
        out_specs=(vmem,) * 4,
        scratch_shapes=[
            pltpu.VMEM((2, SLOTS, width), BF),
            pltpu.VMEM((8, D3 * GROUP, LANES), BF),
            pltpu.VMEM((2 * D1 * D2, LANES, LANES), BF),
            pltpu.VMEM((2, D1 * D2, SLOTS, LANES), BF),
            pltpu.VMEM((D2, 4 * SLOTS, LANES), BF),
            pltpu.VMEM((D2, 4 * SLOTS, LANES), BF),
            pltpu.VMEM((2, D1, SLOTS, LANES), F32),
            pltpu.VMEM((2, SLOTS, SLOTS), BF),
            pltpu.VMEM((8, D1 * GROUP, R), BF),
        ],
        interpret=INTERPRET,
        name="terms",
    )(side, mine, theirs, mid)


R_BLOCK = 16


def mid_copy_kernel(core_ref, out_ref):
    for m in range(4):
        for b in range(D2):
            out_ref[m, b] = core_ref[pl.ds(b * 4 + m, R_BLOCK, stride=4 * D2), :].astype(BF)


def mid_round(core):
    return pl.pallas_call(
        mid_copy_kernel,
        grid=(R // R_BLOCK,),
        out_shape=jax.ShapeDtypeStruct((4, D2, R, LANES), BF),
        in_specs=[pl.BlockSpec((R_BLOCK * D2 * 4, LANES), lambda i: (i, 0))],
        out_specs=pl.BlockSpec((4, D2, R_BLOCK, LANES), lambda i: (0, 0, i, 0)),
        interpret=INTERPRET,
        name="mid_round",
    )(core)


def mid_kernel(
    side_ref, core_ref, moment_ref, second_ref, near_ref, far_ref, near_rest_ref, far_rest_ref,
    core_out, moment_out, second_out, grad,
):
    side = side_ref[0]
    for i in range(2):
        for b in range(D2):
            own = near_ref[i, b].astype(F32) + far_ref[i, b].astype(F32)
            rest = near_rest_ref[i, b].astype(F32) + far_rest_ref[i, b].astype(F32)
            at = b * 4 + i
            grad[pl.ds(at + side * 2, R_BLOCK, stride=4 * D2), :] = own
            grad[pl.ds(at + (1 - side) * 2, R_BLOCK, stride=4 * D2), :] = rest
    core, moment, second = adam_update(core_ref[...], moment_ref[...], second_ref[...], grad[...])
    core_out[...] = core
    moment_out[...] = moment
    second_out[...] = second


def mid_step(side, states, parts):
    rows = R_BLOCK * D2 * 4
    state = pl.BlockSpec((rows, LANES), lambda i: (i, 0))
    part = pl.BlockSpec((2, D2, R_BLOCK, LANES), lambda i: (0, 0, i, 0))
    return pl.pallas_call(
        mid_kernel,
        grid=(R // R_BLOCK,),
        out_shape=tuple(jax.ShapeDtypeStruct(states[0].shape, F32) for _ in range(3)),
        in_specs=[pl.BlockSpec(memory_space=pltpu.SMEM)] + [state] * 3 + [part] * 4,
        out_specs=(state,) * 3,
        scratch_shapes=[pltpu.VMEM((rows, LANES), F32)],
        interpret=INTERPRET,
        name="mid_step",
    )(side, *states, *parts)


def outer_kernel(side_ref, own_ref, chip_ref, core_ref, both_ref, *refs):
    side = side_ref[0]
    mine = own_ref[...] + chip_ref[...]
    theirs = core_ref[...] + both_ref[...]
    first_grad = jnp.where(side == 0, mine, theirs)
    last_grad = jnp.where(side == 0, theirs, mine)
    width = mine.shape[1]
    dest = iota((width, width), 1)
    source = (dest % D3) * LANES + dest // D3
    order = ones_where(iota((width, width), 0) == source)
    hi = last_grad.astype(BF)
    rest = last_grad - hi.astype(F32)
    low, lowest = split_two(rest)
    last_grad = nn(hi, order) + (nn(low, order) + nn(lowest, order))
    f_next = adam_update(refs[0][...], refs[1][...], refs[2][...], first_grad)
    l_next = adam_update(refs[3][...], refs[4][...], refs[5][...], last_grad)
    for ref, value in zip(refs[6:], f_next + l_next):
        ref[...] = value


def outer_step(side, shares, states):
    vmem = pl.BlockSpec(memory_space=pltpu.VMEM)
    mine = shares[0]
    return pl.pallas_call(
        outer_kernel,
        out_shape=tuple(jax.ShapeDtypeStruct(mine.shape, F32) for _ in range(6)),
        in_specs=[pl.BlockSpec(memory_space=pltpu.SMEM)] + [vmem] * 10,
        out_specs=(vmem,) * 6,
        interpret=INTERPRET,
        name="outer",
    )(side, *shares, *states)


def row_tiles(x):
    return x.reshape(4, D2 * R, LANES).transpose(1, 0, 2).reshape(4 * D2 * R, LANES)


def untile(x):
    return x.reshape(D2 * R, 4, LANES).transpose(1, 0, 2).reshape(4, D2 * R * LANES)


CORE_SWAP = ((0, 1), (1, 0), (2, 3), (3, 2))
CHIP_SWAP = ((0, 2), (2, 0), (1, 3), (3, 1))
BOTH_SWAP = ((0, 3), (3, 0), (1, 2), (2, 1))


def local(
    first_core,
    first_moment,
    first_second,
    mid_core,
    mid_moment,
    mid_second,
    last_core,
    last_moment,
    last_second,
    cotangent,
    bag_lengths,
    first_digit,
    mid_digit,
    last_digit,
):
    side = (lax.axis_index("rep") % 2).astype(jnp.int32).reshape(1)
    packed = pack(
        side,
        mid_digit.reshape(1, -1),
        first_digit.reshape(1, -1),
        last_digit.reshape(1, -1),
        bag_lengths,
        cotangent,
        first_core,
        last_core,
    )
    mid_rows = row_tiles(mid_core)
    mine = lax.all_to_all(packed, "dp", split_axis=0, concat_axis=0, tiled=True)
    mid_copy = mid_round(mid_rows)
    theirs = lax.ppermute(mine, "rep", CORE_SWAP)
    mid_keep, mid_send, keep, send = terms(side, mine, theirs, mid_copy)

    mid_other = lax.ppermute(mid_send, "rep", CORE_SWAP)
    other = lax.ppermute(send, "rep", CORE_SWAP)
    near = (mid_keep + mid_other).astype(BF)
    near, chip_sum = lax.optimization_barrier((near, (keep + other).astype(BF)))
    far = lax.ppermute(near, "rep", CHIP_SWAP)
    share = lax.all_to_all(chip_sum, "dp", split_axis=0, concat_axis=0, tiled=True)
    near_rest = lax.ppermute(near, "rep", CORE_SWAP)
    far_rest = lax.ppermute(far, "rep", CORE_SWAP)
    mid_next = mid_step(
        side,
        (mid_rows, row_tiles(mid_moment), row_tiles(mid_second)),
        (near, far, near_rest, far_rest),
    )

    share, *mid_next = lax.optimization_barrier((share, *mid_next))
    mid_next = tuple(untile(x) for x in mid_next)
    share = jnp.sum(share.reshape(N_SRC, -1, share.shape[1]).astype(F32), axis=0)
    swapped = tuple(
        lax.ppermute(share, "rep", pairs) for pairs in (CHIP_SWAP, CORE_SWAP, BOTH_SWAP)
    )
    outer = outer_step(
        side,
        (share,) + swapped,
        (first_core, first_moment, first_second, last_core, last_moment, last_second),
    )
    return outer[:3] + mid_next + outer[3:]


def solution(mesh):
    rows = P("dp", None)
    spread = P(("rep", "dp"), None)
    flat = P(("rep", "dp"))
    return jax.shard_map(
        local,
        mesh=mesh,
        in_specs=(rows,) * 9 + (spread, spread, flat, spread, flat),
        out_specs=(rows,) * 9,
        check_vma=False,
    )
```

```python
import jax
import jax.numpy as jnp
from jax import lax
from jax.experimental import pallas as pl
from jax.experimental.pallas import tpu as pltpu
from jax.sharding import PartitionSpec as P


R = 128
D1 = 4
D2 = 8
D3 = 4
STEP = 20
CAP = 2
LANES = 128
N_SRC = 64
SLOTS = 512
GROUP = 32
GROUPS = 16

LEARN_RATE = 0.01
BETA_ONE = 0.9
BETA_TWO = 0.999
EPSILON = 1e-08

BF = jnp.bfloat16
F32 = jnp.float32
INTERPRET = False


def adam_update(current, moment, second, gradient):
    moment_next = BETA_ONE * moment + (1.0 - BETA_ONE) * gradient
    second_next = BETA_TWO * second + (1.0 - BETA_TWO) * gradient * gradient
    corrected = moment_next * (LEARN_RATE / (1.0 - BETA_ONE**STEP))
    spread = jnp.sqrt(second_next * (1.0 / (1.0 - BETA_TWO**STEP)))
    return (current - corrected / (spread + EPSILON), moment_next, second_next)


def iota(shape, axis):
    return lax.broadcasted_iota(jnp.int32, shape, axis)


def nn(a, b):
    return lax.dot_general(a, b, (((1,), (0,)), ((), ())), preferred_element_type=F32)


def nt(a, b):
    return lax.dot_general(a, b, (((1,), (1,)), ((), ())), preferred_element_type=F32)


def tn(a, b):
    return lax.dot_general(a, b, (((0,), (0,)), ((), ())), preferred_element_type=F32)


def ones_where(cond):
    return jnp.where(cond, 1.0, 0.0).astype(BF)


def split_two(x):
    hi = x.astype(BF)
    return hi, (x - hi.astype(F32)).astype(BF)


def pack_kernel(side_ref, mid_ref, first_ref, last_ref, bag_ref, cot_ref, fcore_ref, lcore_ref, out_ref):
    count = mid_ref.shape[1]
    mids = jnp.broadcast_to(mid_ref[...].astype(F32), (count, count))
    row, col = iota((count, count), 0), iota((count, count), 1)
    mid_column = jnp.sum(jnp.where(row == col, mids, 0.0), axis=1, keepdims=True)
    earlier = (mid_column == mids) & (row < col)
    rank = jnp.sum(jnp.where(earlier, 1.0, 0.0), axis=0, keepdims=True)
    slot = mid_ref[...] * CAP + rank.astype(jnp.int32)
    place = ones_where(iota((SLOTS, count), 0) == slot)

    samples = bag_ref.shape[1]
    lens = jnp.broadcast_to(bag_ref[...].astype(F32), (samples, samples))
    n_row, n_col = iota((samples, samples), 0), iota((samples, samples), 1)
    ends = jnp.sum(jnp.where(n_col <= n_row, lens, 0.0), axis=1, keepdims=True)
    starts = jnp.sum(jnp.where(n_col < n_row, lens, 0.0), axis=1, keepdims=True)
    position = iota((samples, count), 1).astype(F32)
    owner = ones_where((position >= starts) & (position < ends))
    slot_owner = nt(place, owner).astype(BF)
    out_ref[:, 0:LANES] = nn(slot_owner, cot_ref[...]).astype(BF)

    field = iota((LANES, count), 0)
    first, last = first_ref[...], last_ref[...]
    fields = jnp.where(field == 0, first // 32, 0)
    fields = jnp.where(field == 1, first % 32, fields)
    fields = jnp.where(field == 2, last // 32, fields)
    fields = jnp.where(field == 3, last % 32, fields)
    out_ref[:, LANES : 2 * LANES] = nt(place, fields.astype(F32).astype(BF)).astype(BF)

    side = side_ref[0]
    width = fcore_ref.shape[1]
    core = jnp.where(side == 0, fcore_ref[...], lcore_ref[...])
    core = jnp.concatenate([core, core], axis=0).astype(BF)
    dest = iota((width, width), 1)
    source = jnp.where(side == 0, dest, (dest % LANES) * D3 + dest // LANES)
    core = nn(core, ones_where(iota((width, width), 0) == source)).astype(BF)
    for p in range(SLOTS // 16):
        out_ref[p * 16 : p * 16 + 16, 2 * LANES : 2 * LANES + width] = core


def pack(side, mid_digit, first_digit, last_digit, bag, cot, first_core, last_core):
    vmem = pl.BlockSpec(memory_space=pltpu.VMEM)
    return pl.pallas_call(
        pack_kernel,
        out_shape=jax.ShapeDtypeStruct((SLOTS, 2 * LANES + first_core.shape[1]), BF),
        in_specs=[pl.BlockSpec(memory_space=pltpu.SMEM)] + [vmem] * 7,
        out_specs=vmem,
        interpret=INTERPRET,
        name="pack",
    )(side, mid_digit, first_digit, last_digit, bag, cot, first_core, last_core)


def terms_kernel(
    side_ref, mine_ref, theirs_ref, mid_ref,
    midkeep_ref, midsend_ref, keep_ref, send_ref,
    cores, lrows, pick, diag, mix_hi, mix_lo, outer, chosen, asub,
):
    side = side_ref[0]
    cores[side] = mine_ref[:, 2 * LANES :]
    cores[1 - side] = theirs_ref[:, 2 * LANES :]
    up, across = iota((SLOTS, SLOTS), 0), iota((SLOTS, SLOTS), 1)
    source = (up // GROUP % 2) * GROUP + up % GROUP
    slots = nn(ones_where(across == source * 8 + up // (2 * GROUP)), mine_ref[:, 0 : 2 * LANES])
    grads = slots[:, 0:LANES].astype(BF)
    first = slots[:, LANES : LANES + 1] * 32.0 + slots[:, LANES + 1 : LANES + 2]
    last = slots[:, LANES + 2 : LANES + 3] * 32.0 + slots[:, LANES + 3 : LANES + 4]
    across_f = across.astype(F32)
    pick_first = ones_where(across_f == first)
    pick_last = ones_where(across_f == last)
    chosen[side] = pick_first
    chosen[1 - side] = pick_last
    arows = nn(pick_first, cores[0]).astype(BF)
    last_rows = nn(pick_last, cores[1]).astype(BF)
    for q in range(GROUPS):
        for c in range(D3):
            lrows[q, c * GROUP : (c + 1) * GROUP, :] = last_rows[
                q * GROUP : (q + 1) * GROUP, c * LANES : (c + 1) * LANES
            ]
        for a in range(D1):
            asub[q, a * GROUP : (a + 1) * GROUP, :] = arows[
                q * GROUP : (q + 1) * GROUP, a * R : (a + 1) * R
            ]

    pick[...] = jnp.zeros(pick.shape, BF)
    tile_row, tile_lane = iota((16, LANES), 0), iota((16, LANES), 1)
    for ab in range(D1 * D2):
        pick[ab, (ab // 4) * 16 : (ab // 4) * 16 + 16, :] = ones_where(
            tile_row == D3 * (ab % 4) + tile_lane // GROUP
        )
    own = ones_where(iota((SLOTS, 2 * LANES), 0) % GROUP == iota((SLOTS, 2 * LANES), 1) % GROUP)

    def spread(step, carry):
        for part in range(4):
            ab = step * 8 + part * 2
            pair = jnp.concatenate([pick[ab], pick[ab + 1]], axis=1)
            value = nn(grads, pair).astype(BF) * own
            diag[ab] = value[:, 0:LANES]
            diag[ab + 1] = value[:, LANES:]
        return carry

    lax.fori_loop(0, D1 * D2 // 8, spread, 0)

    def row(m, carry):
        left = jnp.concatenate([asub[4 * m + g] for g in range(4)], axis=0)
        totals = [None] * 4
        for b in range(0, D2, 2):
            heads = [
                lax.dot_general(
                    mid_ref[m, b + i], left, (((0,), (1,)), ((), ())), preferred_element_type=F32
                ).astype(BF)
                for i in range(2)
            ]
            for g in range(4):
                q = 4 * m + g
                here = pl.ds(pl.multiple_of(q * GROUP, GROUP), GROUP)
                there = pl.ds(pl.multiple_of(q * D1 * GROUP, D1 * GROUP), D1 * GROUP)
                block = jnp.concatenate(
                    [diag[a * D2 + b + i, here, :] for i in range(2) for a in range(D1)], axis=0
                )
                head = jnp.concatenate([h[:, g * LANES : (g + 1) * LANES] for h in heads], axis=1)
                part = nn(head, block)
                totals[g] = part if totals[g] is None else totals[g] + part
                hi, lo = split_two(nn(block, lrows[q]))
                for i in range(2):
                    mix_hi[b + i, there, :] = hi[i * LANES : (i + 1) * LANES]
                    mix_lo[b + i, there, :] = lo[i * LANES : (i + 1) * LANES]
        for g in range(4):
            here = pl.ds(pl.multiple_of((4 * m + g) * GROUP, GROUP), GROUP)
            total = totals[g].T
            for c in range(D3):
                outer[1 - side, c, here, :] = total[c * GROUP : (c + 1) * GROUP, :]
        return carry

    lax.fori_loop(0, 4, row, 0)

    for n in range(4):
        half = side if n < 2 else 1 - side
        m = half * 2 + n % 2
        grad_ref = midkeep_ref if n < 2 else midsend_ref
        span = pl.ds(pl.multiple_of(m * SLOTS, SLOTS), SLOTS)
        left = jnp.concatenate([asub[4 * m + g] for g in range(4)], axis=0)
        part = None
        for b in range(0, D2, 2):
            hi = jnp.concatenate([mix_hi[b, span, :], mix_hi[b + 1, span, :]], axis=1)
            lo = jnp.concatenate([mix_lo[b, span, :], mix_lo[b + 1, span, :]], axis=1)
            pair = jnp.concatenate([mid_ref[m, b], mid_ref[m, b + 1]], axis=1)
            term = nt(jnp.concatenate([hi, lo], axis=1), jnp.concatenate([pair, pair], axis=1))
            part = term if part is None else part + term
            grad = tn(left, hi)
            grad_ref[n % 2, b] = grad[:, 0:LANES]
            grad_ref[n % 2, b + 1] = grad[:, LANES:]
        for q in range(4):
            for a in range(D1):
                here = pl.ds(pl.multiple_of((4 * m + q) * GROUP, GROUP), GROUP)
                outer[side, a, here, :] = part[(q * D1 + a) * GROUP : (q * D1 + a + 1) * GROUP, :]

    for n, ref in ((1, send_ref), (0, keep_ref)):
        for a in range(0, D1, 2):
            hi, lo = split_two(jnp.concatenate([outer[n, a], outer[n, a + 1]], axis=1))
            ref[:, a * LANES : (a + 2) * LANES] = tn(chosen[n], hi) + tn(chosen[n], lo)


def terms(side, mine, theirs, mid):
    vmem = pl.BlockSpec(memory_space=pltpu.VMEM)
    width = D1 * R
    half = (2, D2, R, LANES)
    return pl.pallas_call(
        terms_kernel,
        out_shape=(
            jax.ShapeDtypeStruct(half, F32),
            jax.ShapeDtypeStruct(half, F32),
            jax.ShapeDtypeStruct((SLOTS, width), F32),
            jax.ShapeDtypeStruct((SLOTS, width), F32),
        ),
        in_specs=[pl.BlockSpec(memory_space=pltpu.SMEM)] + [vmem] * 3,
        out_specs=(vmem,) * 4,
        scratch_shapes=[
            pltpu.VMEM((2, SLOTS, width), BF),
            pltpu.VMEM((GROUPS, D3 * GROUP, LANES), BF),
            pltpu.VMEM((D1 * D2, LANES, LANES), BF),
            pltpu.VMEM((D1 * D2, SLOTS, LANES), BF),
            pltpu.VMEM((D2, 4 * SLOTS, LANES), BF),
            pltpu.VMEM((D2, 4 * SLOTS, LANES), BF),
            pltpu.VMEM((2, D1, SLOTS, LANES), F32),
            pltpu.VMEM((2, SLOTS, SLOTS), BF),
            pltpu.VMEM((GROUPS, D1 * GROUP, R), BF),
        ],
        interpret=INTERPRET,
        name="terms",
    )(side, mine, theirs, mid)


R_BLOCK = 16


def mid_copy_kernel(core_ref, out_ref):
    for m in range(4):
        for b in range(D2):
            out_ref[m, b] = core_ref[pl.ds(b * 4 + m, R_BLOCK, stride=4 * D2), :].astype(BF)


def mid_round(core):
    return pl.pallas_call(
        mid_copy_kernel,
        grid=(R // R_BLOCK,),
        out_shape=jax.ShapeDtypeStruct((4, D2, R, LANES), BF),
        in_specs=[pl.BlockSpec((R_BLOCK * D2 * 4, LANES), lambda i: (i, 0))],
        out_specs=pl.BlockSpec((4, D2, R_BLOCK, LANES), lambda i: (0, 0, i, 0)),
        interpret=INTERPRET,
        name="mid_round",
    )(core)


def mid_kernel(
    side_ref, core_ref, moment_ref, second_ref, near_ref, far_ref, near_rest_ref, far_rest_ref,
    core_out, moment_out, second_out, grad,
):
    side = side_ref[0]
    for i in range(2):
        for b in range(D2):
            own = near_ref[i, b].astype(F32) + far_ref[i, b].astype(F32)
            rest = near_rest_ref[i, b].astype(F32) + far_rest_ref[i, b].astype(F32)
            at = b * 4 + i
            grad[pl.ds(at + side * 2, R_BLOCK, stride=4 * D2), :] = own
            grad[pl.ds(at + (1 - side) * 2, R_BLOCK, stride=4 * D2), :] = rest
    core, moment, second = adam_update(core_ref[...], moment_ref[...], second_ref[...], grad[...])
    core_out[...] = core
    moment_out[...] = moment
    second_out[...] = second


def mid_step(side, states, parts):
    rows = R_BLOCK * D2 * 4
    state = pl.BlockSpec((rows, LANES), lambda i: (i, 0))
    part = pl.BlockSpec((2, D2, R_BLOCK, LANES), lambda i: (0, 0, i, 0))
    return pl.pallas_call(
        mid_kernel,
        grid=(R // R_BLOCK,),
        out_shape=tuple(jax.ShapeDtypeStruct(states[0].shape, F32) for _ in range(3)),
        in_specs=[pl.BlockSpec(memory_space=pltpu.SMEM)] + [state] * 3 + [part] * 4,
        out_specs=(state,) * 3,
        scratch_shapes=[pltpu.VMEM((rows, LANES), F32)],
        interpret=INTERPRET,
        name="mid_step",
    )(side, *states, *parts)


def outer_kernel(side_ref, own_ref, chip_ref, core_ref, both_ref, *refs):
    side = side_ref[0]
    mine = own_ref[...] + chip_ref[...]
    theirs = core_ref[...] + both_ref[...]
    first_grad = jnp.where(side == 0, mine, theirs)
    last_grad = jnp.where(side == 0, theirs, mine)
    width = mine.shape[1]
    dest = iota((width, width), 1)
    source = (dest % D3) * LANES + dest // D3
    order = ones_where(iota((width, width), 0) == source)
    hi = last_grad.astype(BF)
    rest = last_grad - hi.astype(F32)
    low, lowest = split_two(rest)
    last_grad = nn(hi, order) + (nn(low, order) + nn(lowest, order))
    f_next = adam_update(refs[0][...], refs[1][...], refs[2][...], first_grad)
    l_next = adam_update(refs[3][...], refs[4][...], refs[5][...], last_grad)
    for ref, value in zip(refs[6:], f_next + l_next):
        ref[...] = value


def outer_step(side, shares, states):
    vmem = pl.BlockSpec(memory_space=pltpu.VMEM)
    mine = shares[0]
    return pl.pallas_call(
        outer_kernel,
        out_shape=tuple(jax.ShapeDtypeStruct(mine.shape, F32) for _ in range(6)),
        in_specs=[pl.BlockSpec(memory_space=pltpu.SMEM)] + [vmem] * 10,
        out_specs=(vmem,) * 6,
        interpret=INTERPRET,
        name="outer",
    )(side, *shares, *states)


def row_tiles(x):
    return x.reshape(4, D2 * R, LANES).transpose(1, 0, 2).reshape(4 * D2 * R, LANES)


def untile(x):
    return x.reshape(D2 * R, 4, LANES).transpose(1, 0, 2).reshape(4, D2 * R * LANES)


CORE_SWAP = ((0, 1), (1, 0), (2, 3), (3, 2))
CHIP_SWAP = ((0, 2), (2, 0), (1, 3), (3, 1))
BOTH_SWAP = ((0, 3), (3, 0), (1, 2), (2, 1))


def local(
    first_core,
    first_moment,
    first_second,
    mid_core,
    mid_moment,
    mid_second,
    last_core,
    last_moment,
    last_second,
    cotangent,
    bag_lengths,
    first_digit,
    mid_digit,
    last_digit,
):
    side = (lax.axis_index("rep") % 2).astype(jnp.int32).reshape(1)
    packed = pack(
        side,
        mid_digit.reshape(1, -1),
        first_digit.reshape(1, -1),
        last_digit.reshape(1, -1),
        bag_lengths,
        cotangent,
        first_core,
        last_core,
    )
    mid_rows = row_tiles(mid_core)
    mine = lax.all_to_all(packed, "dp", split_axis=0, concat_axis=0, tiled=True)
    mid_copy = mid_round(mid_rows)
    theirs = lax.ppermute(mine, "rep", CORE_SWAP)
    mid_keep, mid_send, keep, send = terms(side, mine, theirs, mid_copy)

    mid_other = lax.ppermute(mid_send, "rep", CORE_SWAP)
    other = lax.ppermute(send, "rep", CORE_SWAP)
    near = (mid_keep + mid_other).astype(BF)
    near, chip_sum = lax.optimization_barrier((near, (keep + other).astype(BF)))
    far = lax.ppermute(near, "rep", CHIP_SWAP)
    share = lax.all_to_all(chip_sum, "dp", split_axis=0, concat_axis=0, tiled=True)
    near_rest = lax.ppermute(near, "rep", CORE_SWAP)
    far_rest = lax.ppermute(far, "rep", CORE_SWAP)
    mid_next = mid_step(
        side,
        (mid_rows, row_tiles(mid_moment), row_tiles(mid_second)),
        (near, far, near_rest, far_rest),
    )

    share, *mid_next = lax.optimization_barrier((share, *mid_next))
    mid_next = tuple(untile(x) for x in mid_next)
    share = jnp.sum(share.reshape(N_SRC, -1, share.shape[1]).astype(F32), axis=0)
    swapped = tuple(
        lax.ppermute(share, "rep", pairs) for pairs in (CHIP_SWAP, CORE_SWAP, BOTH_SWAP)
    )
    outer = outer_step(
        side,
        (share,) + swapped,
        (first_core, first_moment, first_second, last_core, last_moment, last_second),
    )
    return outer[:3] + mid_next + outer[3:]


def solution(mesh):
    rows = P("dp", None)
    spread = P(("rep", "dp"), None)
    flat = P(("rep", "dp"))
    return jax.shard_map(
        local,
        mesh=mesh,
        in_specs=(rows,) * 9 + (spread, spread, flat, spread, flat),
        out_specs=(rows,) * 9,
        check_vma=False,
    )
```

```python
import jax
import jax.numpy as jnp
from jax import lax
from jax.experimental import pallas as pl
from jax.experimental.pallas import tpu as pltpu
from jax.sharding import PartitionSpec as P


R = 128
D1 = 4
D2 = 8
D3 = 4
STEP = 20
CAP = 2
LANES = 128
N_SRC = 64
SLOTS = 512
GROUP = 32
GROUPS = 16

LEARN_RATE = 0.01
BETA_ONE = 0.9
BETA_TWO = 0.999
EPSILON = 1e-08

BF = jnp.bfloat16
F32 = jnp.float32
INTERPRET = False


def adam_update(current, moment, second, gradient):
    moment_next = BETA_ONE * moment + (1.0 - BETA_ONE) * gradient
    second_next = BETA_TWO * second + (1.0 - BETA_TWO) * gradient * gradient
    corrected = moment_next * (LEARN_RATE / (1.0 - BETA_ONE**STEP))
    spread = jnp.sqrt(second_next * (1.0 / (1.0 - BETA_TWO**STEP)))
    return (current - corrected / (spread + EPSILON), moment_next, second_next)


def iota(shape, axis):
    return lax.broadcasted_iota(jnp.int32, shape, axis)


def nn(a, b):
    return lax.dot_general(a, b, (((1,), (0,)), ((), ())), preferred_element_type=F32)


def nt(a, b):
    return lax.dot_general(a, b, (((1,), (1,)), ((), ())), preferred_element_type=F32)


def tn(a, b):
    return lax.dot_general(a, b, (((0,), (0,)), ((), ())), preferred_element_type=F32)


def ones_where(cond):
    return jnp.where(cond, 1.0, 0.0).astype(BF)


def split_two(x):
    hi = x.astype(BF)
    return hi, (x - hi.astype(F32)).astype(BF)


def pack_kernel(side_ref, mid_ref, first_ref, last_ref, bag_ref, cot_ref, fcore_ref, lcore_ref, out_ref):
    count = mid_ref.shape[1]
    mids = jnp.broadcast_to(mid_ref[...].astype(F32), (count, count))
    row, col = iota((count, count), 0), iota((count, count), 1)
    mid_column = jnp.sum(jnp.where(row == col, mids, 0.0), axis=1, keepdims=True)
    earlier = (mid_column == mids) & (row < col)
    rank = jnp.sum(jnp.where(earlier, 1.0, 0.0), axis=0, keepdims=True)
    slot = mid_ref[...] * CAP + rank.astype(jnp.int32)
    place = ones_where(iota((SLOTS, count), 0) == slot)

    samples = bag_ref.shape[1]
    lens = jnp.broadcast_to(bag_ref[...].astype(F32), (samples, samples))
    n_row, n_col = iota((samples, samples), 0), iota((samples, samples), 1)
    ends = jnp.sum(jnp.where(n_col <= n_row, lens, 0.0), axis=1, keepdims=True)
    starts = jnp.sum(jnp.where(n_col < n_row, lens, 0.0), axis=1, keepdims=True)
    position = iota((samples, count), 1).astype(F32)
    owner = ones_where((position >= starts) & (position < ends))
    slot_owner = nt(place, owner).astype(BF)
    out_ref[:, 0:LANES] = nn(slot_owner, cot_ref[...]).astype(BF)

    field = iota((LANES, count), 0)
    first, last = first_ref[...], last_ref[...]
    fields = jnp.where(field == 0, first // 32, 0)
    fields = jnp.where(field == 1, first % 32, fields)
    fields = jnp.where(field == 2, last // 32, fields)
    fields = jnp.where(field == 3, last % 32, fields)
    out_ref[:, LANES : 2 * LANES] = nt(place, fields.astype(F32).astype(BF)).astype(BF)

    side = side_ref[0]
    width = fcore_ref.shape[1]
    core = jnp.where(side == 0, fcore_ref[...], lcore_ref[...])
    core = jnp.concatenate([core, core], axis=0).astype(BF)
    dest = iota((width, width), 1)
    source = jnp.where(side == 0, dest, (dest % LANES) * D3 + dest // LANES)
    core = nn(core, ones_where(iota((width, width), 0) == source)).astype(BF)
    for p in range(SLOTS // 16):
        out_ref[p * 16 : p * 16 + 16, 2 * LANES : 2 * LANES + width] = core


def pack(side, mid_digit, first_digit, last_digit, bag, cot, first_core, last_core):
    vmem = pl.BlockSpec(memory_space=pltpu.VMEM)
    return pl.pallas_call(
        pack_kernel,
        out_shape=jax.ShapeDtypeStruct((SLOTS, 2 * LANES + first_core.shape[1]), BF),
        in_specs=[pl.BlockSpec(memory_space=pltpu.SMEM)] + [vmem] * 7,
        out_specs=vmem,
        interpret=INTERPRET,
        name="pack",
    )(side, mid_digit, first_digit, last_digit, bag, cot, first_core, last_core)


def terms_kernel(
    side_ref, mine_ref, theirs_ref, mid_ref,
    midkeep_ref, midsend_ref, keep_ref, send_ref,
    cores, lrows, pick, diag, mix_hi, mix_lo, outer, chosen, asub,
):
    side = side_ref[0]
    cores[side] = mine_ref[:, 2 * LANES :]
    cores[1 - side] = theirs_ref[:, 2 * LANES :]
    up, across = iota((SLOTS, SLOTS), 0), iota((SLOTS, SLOTS), 1)
    source = (up // GROUP % 2) * GROUP + up % GROUP
    slots = nn(ones_where(across == source * 8 + up // (2 * GROUP)), mine_ref[:, 0 : 2 * LANES])
    grads = slots[:, 0:LANES].astype(BF)
    first = slots[:, LANES : LANES + 1] * 32.0 + slots[:, LANES + 1 : LANES + 2]
    last = slots[:, LANES + 2 : LANES + 3] * 32.0 + slots[:, LANES + 3 : LANES + 4]
    across_f = across.astype(F32)
    pick_first = ones_where(across_f == first)
    pick_last = ones_where(across_f == last)
    chosen[side] = pick_first
    chosen[1 - side] = pick_last
    arows = nn(pick_first, cores[0]).astype(BF)
    last_rows = nn(pick_last, cores[1]).astype(BF)
    for q in range(GROUPS):
        for c in range(D3):
            lrows[q, c * GROUP : (c + 1) * GROUP, :] = last_rows[
                q * GROUP : (q + 1) * GROUP, c * LANES : (c + 1) * LANES
            ]
        for a in range(D1):
            asub[q, a * GROUP : (a + 1) * GROUP, :] = arows[
                q * GROUP : (q + 1) * GROUP, a * R : (a + 1) * R
            ]

    pick[...] = jnp.zeros(pick.shape, BF)
    tile_row, tile_lane = iota((16, LANES), 0), iota((16, LANES), 1)
    for ab in range(D1 * D2):
        pick[ab, (ab // 4) * 16 : (ab // 4) * 16 + 16, :] = ones_where(
            tile_row == D3 * (ab % 4) + tile_lane // GROUP
        )
    own = ones_where(iota((SLOTS, 2 * LANES), 0) % GROUP == iota((SLOTS, 2 * LANES), 1) % GROUP)

    def spread(step, carry):
        for part in range(4):
            ab = step * 8 + part * 2
            pair = jnp.concatenate([pick[ab], pick[ab + 1]], axis=1)
            value = nn(grads, pair).astype(BF) * own
            diag[ab] = value[:, 0:LANES]
            diag[ab + 1] = value[:, LANES:]
        return carry

    lax.fori_loop(0, D1 * D2 // 8, spread, 0)

    def row(m, carry):
        left = jnp.concatenate([asub[4 * m + g] for g in range(4)], axis=0)
        totals = [None] * 4
        for b in range(0, D2, 2):
            heads = [
                lax.dot_general(
                    mid_ref[m, b + i], left, (((0,), (1,)), ((), ())), preferred_element_type=F32
                ).astype(BF)
                for i in range(2)
            ]
            for g in range(4):
                q = 4 * m + g
                here = pl.ds(pl.multiple_of(q * GROUP, GROUP), GROUP)
                there = pl.ds(pl.multiple_of(q * D1 * GROUP, D1 * GROUP), D1 * GROUP)
                block = jnp.concatenate(
                    [diag[a * D2 + b + i, here, :] for i in range(2) for a in range(D1)], axis=0
                )
                head = jnp.concatenate([h[:, g * LANES : (g + 1) * LANES] for h in heads], axis=1)
                part = nn(head, block)
                totals[g] = part if totals[g] is None else totals[g] + part
                hi, lo = split_two(nn(block, lrows[q]))
                for i in range(2):
                    mix_hi[b + i, there, :] = hi[i * LANES : (i + 1) * LANES]
                    mix_lo[b + i, there, :] = lo[i * LANES : (i + 1) * LANES]
        for g in range(4):
            here = pl.ds(pl.multiple_of((4 * m + g) * GROUP, GROUP), GROUP)
            total = totals[g].T
            for c in range(D3):
                outer[1 - side, c, here, :] = total[c * GROUP : (c + 1) * GROUP, :]
        return carry

    lax.fori_loop(0, 4, row, 0)

    for n in range(4):
        half = side if n < 2 else 1 - side
        m = half * 2 + n % 2
        grad_ref = midkeep_ref if n < 2 else midsend_ref
        span = pl.ds(pl.multiple_of(m * SLOTS, SLOTS), SLOTS)
        left = jnp.concatenate([asub[4 * m + g] for g in range(4)], axis=0)
        part = None
        for b in range(0, D2, 2):
            hi = jnp.concatenate([mix_hi[b, span, :], mix_hi[b + 1, span, :]], axis=1)
            lo = jnp.concatenate([mix_lo[b, span, :], mix_lo[b + 1, span, :]], axis=1)
            pair = jnp.concatenate([mid_ref[m, b], mid_ref[m, b + 1]], axis=1)
            term = nt(jnp.concatenate([hi, lo], axis=1), jnp.concatenate([pair, pair], axis=1))
            part = term if part is None else part + term
            grad = tn(left, hi)
            for h in range(2):
                tops = slice(h * (R // 2), (h + 1) * (R // 2))
                grad_ref[h, n % 2, b] = grad[tops, 0:LANES]
                grad_ref[h, n % 2, b + 1] = grad[tops, LANES:]
        for q in range(4):
            for a in range(D1):
                here = pl.ds(pl.multiple_of((4 * m + q) * GROUP, GROUP), GROUP)
                outer[side, a, here, :] = part[(q * D1 + a) * GROUP : (q * D1 + a + 1) * GROUP, :]

    for n, ref in ((1, send_ref), (0, keep_ref)):
        for a in range(0, D1, 2):
            hi, lo = split_two(jnp.concatenate([outer[n, a], outer[n, a + 1]], axis=1))
            ref[:, a * LANES : (a + 2) * LANES] = tn(chosen[n], hi) + tn(chosen[n], lo)


def terms(side, mine, theirs, mid):
    vmem = pl.BlockSpec(memory_space=pltpu.VMEM)
    width = D1 * R
    half = (2, 2, D2, R // 2, LANES)
    return pl.pallas_call(
        terms_kernel,
        out_shape=(
            jax.ShapeDtypeStruct(half, F32),
            jax.ShapeDtypeStruct(half, F32),
            jax.ShapeDtypeStruct((SLOTS, width), F32),
            jax.ShapeDtypeStruct((SLOTS, width), F32),
        ),
        in_specs=[pl.BlockSpec(memory_space=pltpu.SMEM)] + [vmem] * 3,
        out_specs=(vmem,) * 4,
        scratch_shapes=[
            pltpu.VMEM((2, SLOTS, width), BF),
            pltpu.VMEM((GROUPS, D3 * GROUP, LANES), BF),
            pltpu.VMEM((D1 * D2, LANES, LANES), BF),
            pltpu.VMEM((D1 * D2, SLOTS, LANES), BF),
            pltpu.VMEM((D2, 4 * SLOTS, LANES), BF),
            pltpu.VMEM((D2, 4 * SLOTS, LANES), BF),
            pltpu.VMEM((2, D1, SLOTS, LANES), F32),
            pltpu.VMEM((2, SLOTS, SLOTS), BF),
            pltpu.VMEM((GROUPS, D1 * GROUP, R), BF),
        ],
        interpret=INTERPRET,
        name="terms",
    )(side, mine, theirs, mid)


R_BLOCK = 16


def mid_copy_kernel(core_ref, out_ref):
    for m in range(4):
        for b in range(D2):
            out_ref[m, b] = core_ref[pl.ds(b * 4 + m, R_BLOCK, stride=4 * D2), :].astype(BF)


def mid_round(core):
    return pl.pallas_call(
        mid_copy_kernel,
        grid=(R // R_BLOCK,),
        out_shape=jax.ShapeDtypeStruct((4, D2, R, LANES), BF),
        in_specs=[pl.BlockSpec((R_BLOCK * D2 * 4, LANES), lambda i: (i, 0))],
        out_specs=pl.BlockSpec((4, D2, R_BLOCK, LANES), lambda i: (0, 0, i, 0)),
        interpret=INTERPRET,
        name="mid_round",
    )(core)


def mid_kernel(
    side_ref, core_ref, moment_ref, second_ref, near_ref, far_ref, near_rest_ref, far_rest_ref, *refs
):
    core_out, moment_out, second_out, grad = refs[-4:]
    side = side_ref[0]
    for i in range(2):
        for b in range(D2):
            own = near_ref[i, b].astype(F32) + far_ref[i, b].astype(F32)
            rest = near_rest_ref[i, b].astype(F32) + far_rest_ref[i, b].astype(F32)
            at = b * 4 + i
            grad[pl.ds(at + side * 2, R_BLOCK, stride=4 * D2), :] = own
            grad[pl.ds(at + (1 - side) * 2, R_BLOCK, stride=4 * D2), :] = rest
    core, moment, second = adam_update(core_ref[...], moment_ref[...], second_ref[...], grad[...])
    core_out[...] = core
    moment_out[...] = moment
    second_out[...] = second


def mid_step(side, states, parts, h, begun):
    rows = R_BLOCK * D2 * 4
    blocks = R // R_BLOCK // 2
    state = pl.BlockSpec((rows, LANES), lambda i: (i + h * blocks, 0))
    part = pl.BlockSpec((2, D2, R_BLOCK, LANES), lambda i: (0, 0, i, 0))
    untouched = [pl.BlockSpec(memory_space=pl.ANY)] * len(begun)
    return pl.pallas_call(
        mid_kernel,
        grid=(blocks,),
        out_shape=tuple(jax.ShapeDtypeStruct(states[0].shape, F32) for _ in range(3)),
        in_specs=[pl.BlockSpec(memory_space=pltpu.SMEM)] + [state] * 3 + [part] * 4 + untouched,
        out_specs=(state,) * 3,
        input_output_aliases={8 + n: n for n in range(len(begun))},
        scratch_shapes=[pltpu.VMEM((rows, LANES), F32)],
        interpret=INTERPRET,
        name="mid_step",
    )(side, *states, *parts, *begun)


def outer_kernel(side_ref, own_ref, chip_ref, core_ref, both_ref, *refs):
    side = side_ref[0]
    mine = own_ref[...] + chip_ref[...]
    theirs = core_ref[...] + both_ref[...]
    first_grad = jnp.where(side == 0, mine, theirs)
    last_grad = jnp.where(side == 0, theirs, mine)
    width = mine.shape[1]
    dest = iota((width, width), 1)
    source = (dest % D3) * LANES + dest // D3
    order = ones_where(iota((width, width), 0) == source)
    hi = last_grad.astype(BF)
    rest = last_grad - hi.astype(F32)
    low, lowest = split_two(rest)
    moved = nn(jnp.concatenate([hi, low, lowest], axis=0), order)
    count = mine.shape[0]
    last_grad = moved[:count] + (moved[count : 2 * count] + moved[2 * count :])
    f_next = adam_update(refs[0][...], refs[1][...], refs[2][...], first_grad)
    l_next = adam_update(refs[3][...], refs[4][...], refs[5][...], last_grad)
    for ref, value in zip(refs[6:], f_next + l_next):
        ref[...] = value


def outer_step(side, shares, states):
    vmem = pl.BlockSpec(memory_space=pltpu.VMEM)
    mine = shares[0]
    return pl.pallas_call(
        outer_kernel,
        out_shape=tuple(jax.ShapeDtypeStruct(mine.shape, F32) for _ in range(6)),
        in_specs=[pl.BlockSpec(memory_space=pltpu.SMEM)] + [vmem] * 10,
        out_specs=(vmem,) * 6,
        interpret=INTERPRET,
        name="outer",
    )(side, *shares, *states)


def row_tiles(x):
    return x.reshape(4, D2 * R, LANES).transpose(1, 0, 2).reshape(4 * D2 * R, LANES)


def untile(x):
    return x.reshape(D2 * R, 4, LANES).transpose(1, 0, 2).reshape(4, D2 * R * LANES)


CORE_SWAP = ((0, 1), (1, 0), (2, 3), (3, 2))
CHIP_SWAP = ((0, 2), (2, 0), (1, 3), (3, 1))
BOTH_SWAP = ((0, 3), (3, 0), (1, 2), (2, 1))


def local(
    first_core,
    first_moment,
    first_second,
    mid_core,
    mid_moment,
    mid_second,
    last_core,
    last_moment,
    last_second,
    cotangent,
    bag_lengths,
    first_digit,
    mid_digit,
    last_digit,
):
    side = (lax.axis_index("rep") % 2).astype(jnp.int32).reshape(1)
    packed = pack(
        side,
        mid_digit.reshape(1, -1),
        first_digit.reshape(1, -1),
        last_digit.reshape(1, -1),
        bag_lengths,
        cotangent,
        first_core,
        last_core,
    )
    mid_rows = row_tiles(mid_core)
    mine = lax.all_to_all(packed, "dp", split_axis=0, concat_axis=0, tiled=True)
    mid_copy = mid_round(mid_rows)
    theirs = lax.ppermute(mine, "rep", CORE_SWAP)
    mid_keep, mid_send, keep, send = terms(side, mine, theirs, mid_copy)

    mid_other = lax.ppermute(mid_send, "rep", CORE_SWAP)
    other = lax.ppermute(send, "rep", CORE_SWAP)
    near = [(mid_keep[h] + mid_other[h]).astype(BF) for h in range(2)]
    *near, chip_sum = lax.optimization_barrier((*near, (keep + other).astype(BF)))
    states = (mid_rows, row_tiles(mid_moment), row_tiles(mid_second))
    mid_next = ()
    far = []
    for h in range(2):
        far.append(lax.ppermute(near[h], "rep", CHIP_SWAP))
    share = lax.all_to_all(chip_sum, "dp", split_axis=0, concat_axis=0, tiled=True)
    for h in range(2):
        near_rest = lax.ppermute(near[h], "rep", CORE_SWAP)
        far_rest = lax.ppermute(far[h], "rep", CORE_SWAP)
        mid_next = mid_step(side, states, (near[h], far[h], near_rest, far_rest), h, mid_next)

    share, *mid_next = lax.optimization_barrier((share, *mid_next))
    mid_next = tuple(untile(x) for x in mid_next)
    share = jnp.sum(share.reshape(N_SRC, -1, share.shape[1]).astype(F32), axis=0)
    swapped = tuple(
        lax.ppermute(share, "rep", pairs) for pairs in (CHIP_SWAP, CORE_SWAP, BOTH_SWAP)
    )
    outer = outer_step(
        side,
        (share,) + swapped,
        (first_core, first_moment, first_second, last_core, last_moment, last_second),
    )
    return outer[:3] + mid_next + outer[3:]


def solution(mesh):
    rows = P("dp", None)
    spread = P(("rep", "dp"), None)
    flat = P(("rep", "dp"))
    return jax.shard_map(
        local,
        mesh=mesh,
        in_specs=(rows,) * 9 + (spread, spread, flat, spread, flat),
        out_specs=(rows,) * 9,
        check_vma=False,
    )
```

```python
import jax
import jax.numpy as jnp
from jax import lax
from jax.experimental import pallas as pl
from jax.experimental.pallas import tpu as pltpu
from jax.sharding import PartitionSpec as P


R = 128
D1 = 4
D2 = 8
D3 = 4
STEP = 20
CAP = 2
LANES = 128
N_SRC = 64
SLOTS = 512
GROUP = 32
GROUPS = 16
BIG = 80

LEARN_RATE = 0.01
BETA_ONE = 0.9
BETA_TWO = 0.999
EPSILON = 1e-08

BF = jnp.bfloat16
F32 = jnp.float32
INTERPRET = False


def adam_update(current, moment, second, gradient):
    moment_next = BETA_ONE * moment + (1.0 - BETA_ONE) * gradient
    second_next = BETA_TWO * second + (1.0 - BETA_TWO) * gradient * gradient
    corrected = moment_next * (LEARN_RATE / (1.0 - BETA_ONE**STEP))
    spread = jnp.sqrt(second_next * (1.0 / (1.0 - BETA_TWO**STEP)))
    return (current - corrected / (spread + EPSILON), moment_next, second_next)


def iota(shape, axis):
    return lax.broadcasted_iota(jnp.int32, shape, axis)


def nn(a, b):
    return lax.dot_general(a, b, (((1,), (0,)), ((), ())), preferred_element_type=F32)


def nt(a, b):
    return lax.dot_general(a, b, (((1,), (1,)), ((), ())), preferred_element_type=F32)


def tn(a, b):
    return lax.dot_general(a, b, (((0,), (0,)), ((), ())), preferred_element_type=F32)


def ones_where(cond):
    return jnp.where(cond, 1.0, 0.0).astype(BF)


def split_two(x):
    hi = x.astype(BF)
    return hi, (x - hi.astype(F32)).astype(BF)


def pack_kernel(side_ref, mid_ref, first_ref, last_ref, bag_ref, cot_ref, fcore_ref, lcore_ref, out_ref):
    count = mid_ref.shape[1]
    mids = jnp.broadcast_to(mid_ref[...].astype(F32), (count, count))
    row, col = iota((count, count), 0), iota((count, count), 1)
    mid_column = jnp.sum(jnp.where(row == col, mids, 0.0), axis=1, keepdims=True)
    earlier = (mid_column == mids) & (row < col)
    rank = jnp.sum(jnp.where(earlier, 1.0, 0.0), axis=0, keepdims=True)
    slot = mid_ref[...] * CAP + rank.astype(jnp.int32)
    place = ones_where(iota((SLOTS, count), 0) == slot)

    samples = bag_ref.shape[1]
    lens = jnp.broadcast_to(bag_ref[...].astype(F32), (samples, samples))
    n_row, n_col = iota((samples, samples), 0), iota((samples, samples), 1)
    ends = jnp.sum(jnp.where(n_col <= n_row, lens, 0.0), axis=1, keepdims=True)
    starts = jnp.sum(jnp.where(n_col < n_row, lens, 0.0), axis=1, keepdims=True)
    position = iota((samples, count), 1).astype(F32)
    owner = ones_where((position >= starts) & (position < ends))
    slot_owner = nt(place, owner).astype(BF)
    out_ref[:, 0:LANES] = nn(slot_owner, cot_ref[...]).astype(BF)

    field = iota((LANES, count), 0)
    first, last = first_ref[...], last_ref[...]
    fields = jnp.where(field == 0, first // 32, 0)
    fields = jnp.where(field == 1, first % 32, fields)
    fields = jnp.where(field == 2, last // 32, fields)
    fields = jnp.where(field == 3, last % 32, fields)
    out_ref[:, LANES : 2 * LANES] = nt(place, fields.astype(F32).astype(BF)).astype(BF)

    side = side_ref[0]
    width = fcore_ref.shape[1]
    core = jnp.where(side == 0, fcore_ref[...], lcore_ref[...])
    core = jnp.concatenate([core, core], axis=0).astype(BF)
    dest = iota((width, width), 1)
    source = jnp.where(side == 0, dest, (dest % LANES) * D3 + dest // LANES)
    core = nn(core, ones_where(iota((width, width), 0) == source)).astype(BF)
    for p in range(SLOTS // 16):
        out_ref[p * 16 : p * 16 + 16, 2 * LANES : 2 * LANES + width] = core


def pack(side, mid_digit, first_digit, last_digit, bag, cot, first_core, last_core):
    vmem = pl.BlockSpec(memory_space=pltpu.VMEM)
    return pl.pallas_call(
        pack_kernel,
        out_shape=jax.ShapeDtypeStruct((SLOTS, 2 * LANES + first_core.shape[1]), BF),
        in_specs=[pl.BlockSpec(memory_space=pltpu.SMEM)] + [vmem] * 7,
        out_specs=vmem,
        interpret=INTERPRET,
        name="pack",
    )(side, mid_digit, first_digit, last_digit, bag, cot, first_core, last_core)


def terms_kernel(
    side_ref, mine_ref, theirs_ref, mid_ref,
    keep_big, keep_small, send_big, send_small, keep_ref, send_ref,
    cores, lrows, pick, diag, mix_hi, mix_lo, outer, chosen, asub,
):
    side = side_ref[0]
    cores[side] = mine_ref[:, 2 * LANES :]
    cores[1 - side] = theirs_ref[:, 2 * LANES :]
    up, across = iota((SLOTS, SLOTS), 0), iota((SLOTS, SLOTS), 1)
    source = (up // GROUP % 2) * GROUP + up % GROUP
    slots = nn(ones_where(across == source * 8 + up // (2 * GROUP)), mine_ref[:, 0 : 2 * LANES])
    grads = slots[:, 0:LANES].astype(BF)
    first = slots[:, LANES : LANES + 1] * 32.0 + slots[:, LANES + 1 : LANES + 2]
    last = slots[:, LANES + 2 : LANES + 3] * 32.0 + slots[:, LANES + 3 : LANES + 4]
    across_f = across.astype(F32)
    pick_first = ones_where(across_f == first)
    pick_last = ones_where(across_f == last)
    chosen[side] = pick_first
    chosen[1 - side] = pick_last
    arows = nn(pick_first, cores[0]).astype(BF)
    last_rows = nn(pick_last, cores[1]).astype(BF)
    for q in range(GROUPS):
        for c in range(D3):
            lrows[q, c * GROUP : (c + 1) * GROUP, :] = last_rows[
                q * GROUP : (q + 1) * GROUP, c * LANES : (c + 1) * LANES
            ]
        for a in range(D1):
            asub[q, a * GROUP : (a + 1) * GROUP, :] = arows[
                q * GROUP : (q + 1) * GROUP, a * R : (a + 1) * R
            ]

    pick[...] = jnp.zeros(pick.shape, BF)
    tile_row, tile_lane = iota((16, LANES), 0), iota((16, LANES), 1)
    for ab in range(D1 * D2):
        pick[ab, (ab // 4) * 16 : (ab // 4) * 16 + 16, :] = ones_where(
            tile_row == D3 * (ab % 4) + tile_lane // GROUP
        )
    own = ones_where(iota((SLOTS, 2 * LANES), 0) % GROUP == iota((SLOTS, 2 * LANES), 1) % GROUP)

    def spread(step, carry):
        for part in range(4):
            ab = step * 8 + part * 2
            pair = jnp.concatenate([pick[ab], pick[ab + 1]], axis=1)
            value = nn(grads, pair).astype(BF) * own
            diag[ab] = value[:, 0:LANES]
            diag[ab + 1] = value[:, LANES:]
        return carry

    lax.fori_loop(0, D1 * D2 // 8, spread, 0)

    def row(m, carry):
        left = jnp.concatenate([asub[4 * m + g] for g in range(4)], axis=0)
        totals = [None] * 4
        for b in range(0, D2, 2):
            heads = [
                lax.dot_general(
                    mid_ref[m, b + i], left, (((0,), (1,)), ((), ())), preferred_element_type=F32
                ).astype(BF)
                for i in range(2)
            ]
            for g in range(4):
                q = 4 * m + g
                here = pl.ds(pl.multiple_of(q * GROUP, GROUP), GROUP)
                there = pl.ds(pl.multiple_of(q * D1 * GROUP, D1 * GROUP), D1 * GROUP)
                block = jnp.concatenate(
                    [diag[a * D2 + b + i, here, :] for i in range(2) for a in range(D1)], axis=0
                )
                head = jnp.concatenate([h[:, g * LANES : (g + 1) * LANES] for h in heads], axis=1)
                part = nn(head, block)
                totals[g] = part if totals[g] is None else totals[g] + part
                hi, lo = split_two(nn(block, lrows[q]))
                for i in range(2):
                    mix_hi[b + i, there, :] = hi[i * LANES : (i + 1) * LANES]
                    mix_lo[b + i, there, :] = lo[i * LANES : (i + 1) * LANES]
        for g in range(4):
            here = pl.ds(pl.multiple_of((4 * m + g) * GROUP, GROUP), GROUP)
            total = totals[g].T
            for c in range(D3):
                outer[1 - side, c, here, :] = total[c * GROUP : (c + 1) * GROUP, :]
        return carry

    lax.fori_loop(0, 4, row, 0)

    for n in range(4):
        half = side if n < 2 else 1 - side
        m = half * 2 + n % 2
        grad_refs = (keep_big, keep_small) if n < 2 else (send_big, send_small)
        span = pl.ds(pl.multiple_of(m * SLOTS, SLOTS), SLOTS)
        left = jnp.concatenate([asub[4 * m + g] for g in range(4)], axis=0)
        part = None
        for b in range(0, D2, 2):
            hi = jnp.concatenate([mix_hi[b, span, :], mix_hi[b + 1, span, :]], axis=1)
            lo = jnp.concatenate([mix_lo[b, span, :], mix_lo[b + 1, span, :]], axis=1)
            pair = jnp.concatenate([mid_ref[m, b], mid_ref[m, b + 1]], axis=1)
            term = nt(jnp.concatenate([hi, lo], axis=1), jnp.concatenate([pair, pair], axis=1))
            part = term if part is None else part + term
            grad = tn(left, hi)
            for grad_ref, tops in zip(grad_refs, (slice(0, BIG), slice(BIG, R))):
                grad_ref[n % 2, b] = grad[tops, 0:LANES]
                grad_ref[n % 2, b + 1] = grad[tops, LANES:]
        for q in range(4):
            for a in range(D1):
                here = pl.ds(pl.multiple_of((4 * m + q) * GROUP, GROUP), GROUP)
                outer[side, a, here, :] = part[(q * D1 + a) * GROUP : (q * D1 + a + 1) * GROUP, :]

    for n, ref in ((1, send_ref), (0, keep_ref)):
        for a in range(0, D1, 2):
            hi, lo = split_two(jnp.concatenate([outer[n, a], outer[n, a + 1]], axis=1))
            ref[:, a * LANES : (a + 2) * LANES] = tn(chosen[n], hi) + tn(chosen[n], lo)


def terms(side, mine, theirs, mid):
    vmem = pl.BlockSpec(memory_space=pltpu.VMEM)
    width = D1 * R
    big, small = (2, D2, BIG, LANES), (2, D2, R - BIG, LANES)
    return pl.pallas_call(
        terms_kernel,
        out_shape=(
            jax.ShapeDtypeStruct(big, F32),
            jax.ShapeDtypeStruct(small, F32),
            jax.ShapeDtypeStruct(big, F32),
            jax.ShapeDtypeStruct(small, F32),
            jax.ShapeDtypeStruct((SLOTS, width), F32),
            jax.ShapeDtypeStruct((SLOTS, width), F32),
        ),
        in_specs=[pl.BlockSpec(memory_space=pltpu.SMEM)] + [vmem] * 3,
        out_specs=(vmem,) * 6,
        scratch_shapes=[
            pltpu.VMEM((2, SLOTS, width), BF),
            pltpu.VMEM((GROUPS, D3 * GROUP, LANES), BF),
            pltpu.VMEM((D1 * D2, LANES, LANES), BF),
            pltpu.VMEM((D1 * D2, SLOTS, LANES), BF),
            pltpu.VMEM((D2, 4 * SLOTS, LANES), BF),
            pltpu.VMEM((D2, 4 * SLOTS, LANES), BF),
            pltpu.VMEM((2, D1, SLOTS, LANES), F32),
            pltpu.VMEM((2, SLOTS, SLOTS), BF),
            pltpu.VMEM((GROUPS, D1 * GROUP, R), BF),
        ],
        interpret=INTERPRET,
        name="terms",
    )(side, mine, theirs, mid)


R_BLOCK = 16


def mid_copy_kernel(core_ref, out_ref):
    for m in range(4):
        for b in range(D2):
            out_ref[m, b] = core_ref[pl.ds(b * 4 + m, R_BLOCK, stride=4 * D2), :].astype(BF)


def mid_round(core):
    return pl.pallas_call(
        mid_copy_kernel,
        grid=(R // R_BLOCK,),
        out_shape=jax.ShapeDtypeStruct((4, D2, R, LANES), BF),
        in_specs=[pl.BlockSpec((R_BLOCK * D2 * 4, LANES), lambda i: (i, 0))],
        out_specs=pl.BlockSpec((4, D2, R_BLOCK, LANES), lambda i: (0, 0, i, 0)),
        interpret=INTERPRET,
        name="mid_round",
    )(core)


def mid_kernel(
    side_ref, core_ref, moment_ref, second_ref, near_ref, far_ref, near_rest_ref, far_rest_ref, *refs
):
    core_out, moment_out, second_out, grad = refs[-4:]
    side = side_ref[0]
    for i in range(2):
        for b in range(D2):
            own = near_ref[i, b].astype(F32) + far_ref[i, b].astype(F32)
            rest = near_rest_ref[i, b].astype(F32) + far_rest_ref[i, b].astype(F32)
            at = b * 4 + i
            grad[pl.ds(at + side * 2, R_BLOCK, stride=4 * D2), :] = own
            grad[pl.ds(at + (1 - side) * 2, R_BLOCK, stride=4 * D2), :] = rest
    core, moment, second = adam_update(core_ref[...], moment_ref[...], second_ref[...], grad[...])
    core_out[...] = core
    moment_out[...] = moment
    second_out[...] = second


def mid_step(side, states, parts, h, begun):
    rows = R_BLOCK * D2 * 4
    blocks = (R - BIG if h else BIG) // R_BLOCK
    state = pl.BlockSpec((rows, LANES), lambda i: (i + h * (BIG // R_BLOCK), 0))
    part = pl.BlockSpec((2, D2, R_BLOCK, LANES), lambda i: (0, 0, i, 0))
    untouched = [pl.BlockSpec(memory_space=pl.ANY)] * len(begun)
    return pl.pallas_call(
        mid_kernel,
        grid=(blocks,),
        out_shape=tuple(jax.ShapeDtypeStruct(states[0].shape, F32) for _ in range(3)),
        in_specs=[pl.BlockSpec(memory_space=pltpu.SMEM)] + [state] * 3 + [part] * 4 + untouched,
        out_specs=(state,) * 3,
        input_output_aliases={8 + n: n for n in range(len(begun))},
        scratch_shapes=[pltpu.VMEM((rows, LANES), F32)],
        interpret=INTERPRET,
        name="mid_step",
    )(side, *states, *parts, *begun)


def outer_kernel(side_ref, own_ref, chip_ref, core_ref, both_ref, *refs):
    side = side_ref[0]
    mine = own_ref[...] + chip_ref[...]
    theirs = core_ref[...] + both_ref[...]
    first_grad = jnp.where(side == 0, mine, theirs)
    last_grad = jnp.where(side == 0, theirs, mine)
    width = mine.shape[1]
    dest = iota((width, width), 1)
    source = (dest % D3) * LANES + dest // D3
    order = ones_where(iota((width, width), 0) == source)
    hi = last_grad.astype(BF)
    rest = last_grad - hi.astype(F32)
    low, lowest = split_two(rest)
    moved = nn(jnp.concatenate([hi, low, lowest], axis=0), order)
    count = mine.shape[0]
    last_grad = moved[:count] + (moved[count : 2 * count] + moved[2 * count :])
    f_next = adam_update(refs[0][...], refs[1][...], refs[2][...], first_grad)
    l_next = adam_update(refs[3][...], refs[4][...], refs[5][...], last_grad)
    for ref, value in zip(refs[6:], f_next + l_next):
        ref[...] = value


def outer_step(side, shares, states):
    vmem = pl.BlockSpec(memory_space=pltpu.VMEM)
    mine = shares[0]
    return pl.pallas_call(
        outer_kernel,
        out_shape=tuple(jax.ShapeDtypeStruct(mine.shape, F32) for _ in range(6)),
        in_specs=[pl.BlockSpec(memory_space=pltpu.SMEM)] + [vmem] * 10,
        out_specs=(vmem,) * 6,
        interpret=INTERPRET,
        name="outer",
    )(side, *shares, *states)


def row_tiles(x):
    return x.reshape(4, D2 * R, LANES).transpose(1, 0, 2).reshape(4 * D2 * R, LANES)


def untile(x):
    return x.reshape(D2 * R, 4, LANES).transpose(1, 0, 2).reshape(4, D2 * R * LANES)


CORE_SWAP = ((0, 1), (1, 0), (2, 3), (3, 2))
CHIP_SWAP = ((0, 2), (2, 0), (1, 3), (3, 1))
BOTH_SWAP = ((0, 3), (3, 0), (1, 2), (2, 1))


def local(
    first_core,
    first_moment,
    first_second,
    mid_core,
    mid_moment,
    mid_second,
    last_core,
    last_moment,
    last_second,
    cotangent,
    bag_lengths,
    first_digit,
    mid_digit,
    last_digit,
):
    side = (lax.axis_index("rep") % 2).astype(jnp.int32).reshape(1)
    packed = pack(
        side,
        mid_digit.reshape(1, -1),
        first_digit.reshape(1, -1),
        last_digit.reshape(1, -1),
        bag_lengths,
        cotangent,
        first_core,
        last_core,
    )
    mid_rows = row_tiles(mid_core)
    mine = lax.all_to_all(packed, "dp", split_axis=0, concat_axis=0, tiled=True)
    mid_copy = mid_round(mid_rows)
    theirs = lax.ppermute(mine, "rep", CORE_SWAP)
    *mids, keep, send = terms(side, mine, theirs, mid_copy)

    mid_other = [lax.ppermute(x, "rep", CORE_SWAP) for x in mids[2:]]
    other = lax.ppermute(send, "rep", CORE_SWAP)
    near = [(mids[h] + mid_other[h]).astype(BF) for h in range(2)]
    *near, chip_sum = lax.optimization_barrier((*near, (keep + other).astype(BF)))
    states = (mid_rows, row_tiles(mid_moment), row_tiles(mid_second))
    mid_next = ()
    far = []
    for h in range(2):
        far.append(lax.ppermute(near[h], "rep", CHIP_SWAP))
    share = lax.all_to_all(chip_sum, "dp", split_axis=0, concat_axis=0, tiled=True)
    for h in range(2):
        near_rest = lax.ppermute(near[h], "rep", CORE_SWAP)
        far_rest = lax.ppermute(far[h], "rep", CORE_SWAP)
        mid_next = mid_step(side, states, (near[h], far[h], near_rest, far_rest), h, mid_next)

    share, *mid_next = lax.optimization_barrier((share, *mid_next))
    mid_next = tuple(untile(x) for x in mid_next)
    share = jnp.sum(share.reshape(N_SRC, -1, share.shape[1]).astype(F32), axis=0)
    swapped = tuple(
        lax.ppermute(share, "rep", pairs) for pairs in (CHIP_SWAP, CORE_SWAP, BOTH_SWAP)
    )
    outer = outer_step(
        side,
        (share,) + swapped,
        (first_core, first_moment, first_second, last_core, last_moment, last_second),
    )
    return outer[:3] + mid_next + outer[3:]


def solution(mesh):
    rows = P("dp", None)
    spread = P(("rep", "dp"), None)
    flat = P(("rep", "dp"))
    return jax.shard_map(
        local,
        mesh=mesh,
        in_specs=(rows,) * 9 + (spread, spread, flat, spread, flat),
        out_specs=(rows,) * 9,
        check_vma=False,
    )
```
